32 devices in a mesh: clus: 16 (over z, y, x), sub: 2 (over core).
Axes of the slice: x: 2, y: 2, z: 4, core: 2. Of those that a mesh axis runs over, the one named last changes fastest.
Arguments:
- dual_ops: float32 [64, 1536, 1536], P(('clus', 'sub')), may hold values from 0 to 3, as said below
- rigid_modes: float32 [64, 6, 1536], P(('clus', 'sub')), may hold values from -6 to 6
- members: int32 [64, 4, 1536], P(('clus', 'sub')), may hold values from 0 to 6144, as said below
- coarse_inverse: float32 [384, 384], P(('clus', 'sub')), may hold values from -1 to 1
- dual_rhs: float32 [64, 1536, 128], P(('clus', 'sub')), may hold values from -12 to 12
- coarse_rhs: float32 [64, 6, 128], P(('clus', 'sub')), may hold values from -512 to 512
Outputs:
- multipliers: float32 [64, 1536, 128], P(('clus', 'sub'))
- projected: float32 [64, 1536, 128], P(('clus', 'sub'))
The draws below stay inside these ranges and needn't reach their ends.
Inputs may be any that keep to these rules, and one draw needn't show every extreme that they name: Every slot's group lists the slot itself first (its own position (s % 2) * 1536 + i), holds 1 to 4 slots of different subdomains, and is the same set for every slot in it; the group of every slot i >= 256 is that slot and one slot >= 256 of the other subdomain of the same device (members[s, 2:, i] = EMPTY); exported entries name only slots among the first 256 of a subdomain on devices with o in 0, 1, 2 that exist. Number the exported slots of a device k = 256 j + i for slot i of its j-th subdomain, and let E = 512: those with k < E / 4 are named only by groups of the other device of the same cluster; E / 4 <= k < E / 2 only by the device of cluster c + 1 with the same t; E / 2 <= k < 3 E / 4 only by the device of cluster c - 1 with the same t; 3 E / 4 <= k < 7 E / 8 only by the other device of the same cluster and the devices of cluster c + 1; 7 E / 8 <= k only by the other device of the same cluster and the devices of cluster c - 1. In each dual_ops[s] every row's off-diagonal entries sum in magnitude to less than its diagonal entry.
All inputs are finite; a program needn't handle non-finite values.
Results may differ from the reference program's by a relative error of at most 0.00015.
Values sent between devices are 32-bit elements; how exact they have to be, the bound alone decides.
A program may use at most 128 MiB of HBM per device.

```python
import math
import jax
import jax.numpy as jnp
from jax import lax

M = 1536
ESUB = 256
K = 4
NRB = 6
SUB_DEV = 2
NRHS = 128
ITERS = 2
SUBS = 64
NC = 384
N_CLUS = 16
N_SUB = 2


def perm_rows(key, count, length):
    streams = jax.random.split(key, count)
    return jax.vmap(lambda single: jax.random.permutation(single, length))(streams).astype(jnp.int32)


def inverse_rows(table):
    return jnp.argsort(table, axis=-1).astype(jnp.int32)


def take_rows(table, index):
    return jnp.take_along_axis(table, index, axis=1)


def draw_members(key, part):
    export_rows = SUB_DEV * ESUB
    quarter = export_rows // 4
    eighth = export_rows // 8
    local_rows = SUB_DEV * M
    pad_index = local_rows + 6 * export_rows
    inner_slots = M - ESUB
    devices = N_CLUS * N_SUB
    streams = jax.random.split(jax.random.fold_in(key, 7), 4)
    side_order = perm_rows(streams[0], N_CLUS, quarter)
    side_back = inverse_rows(side_order)
    face_order = perm_rows(streams[1], N_CLUS, quarter)
    face_back = inverse_rows(face_order)
    corner = perm_rows(streams[2], 4 * N_CLUS, eighth).reshape(N_CLUS, 4, eighth)
    corner_back = inverse_rows(corner)
    pair_order = perm_rows(streams[3], devices * (SUB_DEV // 2), inner_slots).reshape(devices, SUB_DEV // 2, inner_slots)
    pair_back = inverse_rows(pair_order)
    device = jnp.arange(devices, dtype=jnp.int32)
    cluster = device // N_SUB
    half_index = device % N_SUB
    other_half = 1 - half_index
    lower_cluster = jnp.maximum(cluster - 1, 0)
    has_upper = (cluster < N_CLUS - 1)[:, None]
    has_lower = (cluster > 0)[:, None]
    up_start = 3 * quarter
    down_start = 3 * quarter + eighth

    def base(offset, which):
        value = local_rows + (2 * offset + which) * export_rows + jnp.zeros_like(device)
        return value.astype(jnp.int32)[:, None]

    def own_slots(first, count):
        position = first + jnp.arange(count, dtype=jnp.int32)
        return jnp.broadcast_to((position // ESUB * M + position % ESUB)[None, :], (devices, count))

    def padded(count):
        return jnp.full((devices, count), pad_index, jnp.int32)
    side_partner = jnp.where(half_index[:, None] == 0, side_order[cluster], side_back[cluster])
    part_side = jnp.stack([own_slots(0, quarter), base(1, other_half) + side_partner, padded(quarter), padded(quarter)], -1)
    upper_face = jnp.where(has_upper, base(2, half_index) + 2 * quarter + face_order[cluster], pad_index)
    part_up = jnp.stack([own_slots(quarter, quarter), upper_face, padded(quarter), padded(quarter)], -1)
    lower_face = jnp.where(has_lower, base(0, half_index) + quarter + face_back[lower_cluster], pad_index)
    part_down = jnp.stack([own_slots(2 * quarter, quarter), lower_face, padded(quarter), padded(quarter)], -1)
    group_up = corner_back[cluster, half_index]
    corner_up = jnp.stack([own_slots(up_start, eighth), base(1, other_half) + up_start + take_rows(corner[cluster, other_half], group_up), jnp.where(has_upper, base(2, 0) + down_start + take_rows(corner[cluster, 2], group_up), pad_index), jnp.where(has_upper, base(2, 1) + down_start + take_rows(corner[cluster, 3], group_up), pad_index)], -1)
    group_down = corner_back[lower_cluster, 2 + half_index]
    corner_down = jnp.stack([own_slots(down_start, eighth), jnp.where(has_lower, base(1, other_half) + down_start + take_rows(corner[lower_cluster, 3 - half_index], group_down), pad_index), jnp.where(has_lower, base(0, 0) + up_start + take_rows(corner[lower_cluster, 0], group_down), pad_index), jnp.where(has_lower, base(0, 1) + up_start + take_rows(corner[lower_cluster, 1], group_down), pad_index)], -1)
    exported = jnp.concatenate([part_side, part_up, part_down, corner_up, corner_down], axis=1)
    exported = exported.reshape(devices, SUB_DEV, ESUB, 4)
    subdomain = jnp.arange(SUB_DEV, dtype=jnp.int32)
    even_sub = (subdomain % 2 == 0)[None, :, None]
    partner_slot = jnp.where(even_sub, pair_order[:, subdomain // 2, :], pair_back[:, subdomain // 2, :])
    partner_sub = jnp.where(subdomain % 2 == 0, subdomain + 1, subdomain - 1)[None, :, None]
    slot_index = jnp.arange(inner_slots, dtype=jnp.int32)[None, None, :]
    own_inner = jnp.broadcast_to(subdomain[None, :, None] * M + ESUB + slot_index, (devices, SUB_DEV, inner_slots))
    partner_inner = partner_sub * M + ESUB + partner_slot
    fill_inner = jnp.full((devices, SUB_DEV, inner_slots), pad_index, jnp.int32)
    internal = jnp.stack([own_inner, partner_inner, fill_inner, fill_inner], -1)
    whole = jnp.concatenate([exported, internal], axis=2).reshape(SUBS, M, 4)
    return jnp.transpose(whole, (0, 2, 1)).astype(jnp.int32)


def draw_dual_ops(key, part):
    streams = jax.random.split(jax.random.fold_in(key, 3), 2)
    position = jnp.arange(M, dtype=jnp.float32)
    distance = jnp.abs(position[:, None] - position[None, :])
    level = 0.8 / (1.5 * 512.0 * math.log(1.0 + M / 512.0))
    envelope = level / (1.0 + distance / 256.0)
    on_diagonal = distance == 0.0

    def one_operator(index):
        diagonal = jax.random.uniform(jax.random.fold_in(streams[0], index), (M, 1), jnp.float32, 1.0, 3.0)
        rough = jax.random.uniform(jax.random.fold_in(streams[1], index), (M, M), jnp.float32, -1.0, 1.0)
        return jnp.where(on_diagonal, diagonal, envelope * (1.0 + 0.5 * rough))
    return lax.map(one_operator, jnp.arange(SUBS, dtype=jnp.int32))


def draw_coarse_inverse(key, part):
    streams = jax.random.split(jax.random.fold_in(key, 5), 2)
    diagonal = jax.random.uniform(streams[0], (NC, 1), jnp.float32, 1.0, 2.0)
    spread = jax.random.uniform(streams[1], (NC, NC), jnp.float32, -1.0, 1.0) * math.sqrt(3.0)
    spread = spread * (0.5 / math.sqrt(NC))
    index = jnp.arange(NC, dtype=jnp.int32)
    identity = (index[:, None] == index[None, :]).astype(jnp.float32)
    return 2.0 / M * (identity * diagonal + (1.0 - identity) * spread)


def draw_dual_rhs(key, part):
    stream = jax.random.fold_in(key, 9)
    ramp = (jnp.arange(SUBS, dtype=jnp.float32) / max(SUBS - 1, 1))[:, None, None]
    values = jax.random.truncated_normal(stream, -4.0, 4.0, (SUBS, M, NRHS), jnp.float32)
    return values * (1.0 + 2.0 * ramp)


def block_scale(stream_key, extent, pieces, smallest, high):
    loudness = 1.0
    for dim, blocks in pieces:
        heights = jax.random.uniform(jax.random.fold_in(jax.random.fold_in(stream_key, 6), dim), (blocks,), jnp.float32, smallest / len(pieces), high / len(pieces))
        loudness = loudness * jnp.repeat(jnp.exp(heights), extent[dim] // blocks).reshape((-1,) + (1,) * (len(extent) - 1 - dim))
    return loudness


def normal_values(key, extent, deviation, most, pieces=(), kind=jnp.bfloat16):
    array = jax.random.normal(key, extent, jnp.float32) * deviation
    if len(pieces) > 0:
        array = block_scale(key, extent, pieces, -0.22, 0.18) * array
    return jnp.clip(array, min=-most, max=most).astype(kind)


def setup_inputs(seed: int = 0) -> dict:
    seeds = jax.random.split(jax.random.key(seed), 7)
    dual_ops = draw_dual_ops(jax.random.fold_in(seeds[6], 71), 0)
    rigid_modes = normal_values(seeds[1], (SUBS, NRB, M), 1.0, 6.0, ((0, 32),), jnp.float32)
    members = draw_members(jax.random.fold_in(seeds[6], 71), 0)
    coarse_inverse = draw_coarse_inverse(jax.random.fold_in(seeds[6], 71), 0)
    dual_rhs = draw_dual_rhs(jax.random.fold_in(seeds[6], 71), 0)
    coarse_rhs = normal_values(seeds[5], (SUBS, NRB, NRHS), (M // 16), 512.0, ((0, 32),), jnp.float32)
    return dict(dual_ops=dual_ops, rigid_modes=rigid_modes, members=members, coarse_inverse=coarse_inverse, dual_rhs=dual_rhs, coarse_rhs=coarse_rhs)


def reference(dual_ops, rigid_modes, members, coarse_inverse, dual_rhs, coarse_rhs):
    devices = N_CLUS * N_SUB
    local_rows = SUB_DEV * M
    export_rows = SUB_DEV * ESUB
    pad_index = local_rows + 6 * export_rows
    slots_all = SUBS * M
    tables = jnp.transpose(members.reshape(devices, SUB_DEV, K, M), (2, 0, 1, 3)).reshape(K, devices, local_rows)
    device = jnp.arange(devices, dtype=jnp.int32)[None, :, None]
    offset = tables - local_rows
    cycle_block = offset // export_rows
    within = offset % export_rows
    target = (device // N_SUB + cycle_block // 2 - 1) * N_SUB + cycle_block % 2
    remote = target * local_rows + (within // ESUB) * M + within % ESUB
    global_slot = jnp.where(tables < local_rows, device * local_rows + tables,
                            jnp.where(tables >= pad_index, slots_all, remote))
    global_slot = global_slot.reshape(K, slots_all).astype(jnp.int32)
    group_size = jnp.sum((global_slot < slots_all).astype(jnp.float32), axis=0)[:, None]
    empty_row = jnp.zeros((1, NRHS), jnp.float32)

    def jump_part(field):
        flat_field = field.reshape(slots_all, NRHS)
        pool_rows = jnp.concatenate([flat_field, empty_row], axis=0)
        group_total = jnp.take(pool_rows, global_slot[0], axis=0)
        for member in range(1, K):
            group_total = group_total + jnp.take(pool_rows, global_slot[member], axis=0)
        return (flat_field - group_total / group_size).reshape(field.shape)

    def blockwise(field):
        return jnp.einsum("smq,sqn->smn", dual_ops, field, precision=lax.Precision.HIGHEST)

    def lift(coarse):
        weights = jnp.dot(coarse_inverse, coarse, precision=lax.Precision.HIGHEST, preferred_element_type=jnp.float32)
        weights = weights.reshape(SUBS, NRB, NRHS)
        return jump_part(jnp.einsum("skm,skn->smn", rigid_modes, weights, precision=lax.Precision.HIGHEST))

    def restrict(field):
        return jnp.einsum("skm,smn->skn", rigid_modes, field, precision=lax.Precision.HIGHEST).reshape(NC, NRHS)

    def project(field):
        return field - lift(restrict(field))

    multipliers = lift(coarse_rhs.reshape(NC, NRHS))
    residual_now = jump_part(dual_rhs - blockwise(multipliers))
    projected = project(residual_now)
    direction = projected
    norm_now = jnp.sum(projected * projected, axis=(0, 1))
    for iteration in range(ITERS):
        along = jump_part(blockwise(direction))
        step_size = norm_now / jnp.sum(direction * along, axis=(0, 1))
        multipliers = multipliers + step_size[None, None, :] * direction
        residual_now = residual_now - step_size[None, None, :] * along
        projected = project(residual_now)
        if iteration + 1 < ITERS:
            norm_next = jnp.sum(projected * projected, axis=(0, 1))
            direction = projected + (norm_next / norm_now)[None, None, :] * direction
            norm_now = norm_next
    return multipliers, projected
```

```python
import functools
import jax
import jax.numpy as jnp
from jax import lax
from jax.experimental import pallas as pl
from jax.experimental.pallas import tpu as pltpu
from jax.sharding import PartitionSpec as P

ESUB = 256
LANES = 128
TILE = 256
POOL = 768
ROUNDS = 4
HALOS = 5
BUFS = 4
REACH = 5
MESH = pl.DeviceIdType.MESH
F32 = jnp.float32
BF16 = jnp.bfloat16


def halves(value):
    high = value.astype(BF16)
    return high, (value - high.astype(F32)).astype(BF16)


def split(value):
    return jnp.concatenate(halves(value), axis=1)


def mm(left, right):
    return jnp.dot(left, right, preferred_element_type=F32)


def fold(wide):
    return wide[:, :LANES] + wide[:, LANES:]


def row_sum(value):
    return jnp.sum(value, axis=0, keepdims=True)


def kernel(
    ops_hbm, modes_in, members, cinv, rhs_hbm, crhs,
    mult, proj,
    ops_hi, ops_lo, ops_buf, perm0, perm1, share, lift_cat, image_cat, c1_cat, cat, cat2,
    image, field, jumped, past, pool, coarse, near, near_cat, modes, outer, columns,
    ops_sem, rhs_sem, halo_send, halo_recv, near_send, near_recv, ag_send, ag_recv, fwd_send, fwd_recv,
    *, clusters,
):
    c = lax.axis_index("clus")
    t = lax.axis_index("sub")
    other = 1 - t
    has_up = c < clusters - 1
    has_down = c > 0
    has_up2 = c < clusters - 2
    has_down2 = c > 1
    up = jnp.minimum(c + 1, clusters - 1)
    down = jnp.maximum(c - 1, 0)
    up2 = jnp.minimum(c + 2, clusters - 1)
    down2 = jnp.maximum(c - 2, 0)
    slot = (c % REACH) * 2 + t
    rows = ops_hi.shape[1]
    total = 2 * rows
    inner = rows - ESUB
    per = rows // TILE
    count = 2 * modes_in.shape[0]
    edges = (0, rows)
    inners = [start for n in range(1, per) for start in (n * TILE, rows + n * TILE)]

    def chunk_home(chunk):
        return chunk % 2, pl.multiple_of((chunk // 2) * TILE, TILE)

    def load(chunk, buf):
        sub, start = chunk_home(chunk)
        return pltpu.make_async_copy(ops_hbm.at[sub, pl.ds(start, TILE)], ops_buf.at[buf], ops_sem.at[buf])

    def halo_copies(source, r):
        plan = [
            (0, 128, 0, (c, other)),
            (rows + 128, 128, 128, (c, other)),
            (128, 128, 256, (up, t)),
            (rows + 128, 64, 384, (up, t)),
            (rows + 128, 64, 640, (up, other)),
            (rows, 128, 448, (down, t)),
            (rows + 192, 64, 576, (down, t)),
            (rows + 192, 64, 704, (down, other)),
        ]
        copies = [
            pltpu.make_async_remote_copy(
                src_ref=source.at[pl.ds(start, size)],
                dst_ref=pool.at[r, pl.ds(to, size)],
                send_sem=halo_send.at[r, n],
                recv_sem=halo_recv.at[r, n],
                device_id=device,
                device_id_type=MESH,
            )
            for n, (start, size, to, device) in enumerate(plan)
        ]
        return [
            (None, None, copies[:2]),
            (has_up, has_down, copies[2:5]),
            (has_down, has_up, copies[5:]),
        ]

    def near_copies():
        plan = [
            (c, other), (up, t), (up, other), (down, t), (down, other),
            (up2, t), (up2, other), (down2, t), (down2, other),
        ]
        copies = [
            pltpu.make_async_remote_copy(
                src_ref=cinv,
                dst_ref=near.at[slot],
                send_sem=near_send.at[n],
                recv_sem=near_recv.at[n],
                device_id=device,
                device_id_type=MESH,
            )
            for n, device in enumerate(plan)
        ]
        return [
            (None, None, copies[:1]),
            (has_up, has_down, copies[1:3]),
            (has_down, has_up, copies[3:5]),
            (has_up2, has_down2, copies[5:7]),
            (has_down2, has_up2, copies[7:9]),
        ]

    def guarded(condition, action):
        if condition is None:
            action()
        else:
            pl.when(condition)(action)

    def start_all(groups):
        for sends, _, copies in reversed(groups):
            def go(copies=copies):
                for copy in copies:
                    copy.start()

            guarded(sends, go)

    def wait_all(groups):
        for sends, receives, copies in groups:
            def sent(copies=copies):
                for copy in copies:
                    copy.wait_send()

            def received(copies=copies):
                for copy in copies:
                    copy.wait_recv()

            guarded(sends, sent)
            guarded(receives, received)

    def ag_copy(r, k):
        return pltpu.make_async_remote_copy(
            src_ref=coarse.at[r, t, c],
            dst_ref=coarse.at[r, t, c],
            send_sem=ag_send.at[r, k],
            recv_sem=ag_recv.at[r, k],
            device_id=((c + k) % clusters, t),
            device_id_type=MESH,
        )

    def ag_arrival(r, k):
        source = (c + clusters - k) % clusters
        return pltpu.make_async_remote_copy(
            src_ref=coarse.at[r, t, source],
            dst_ref=coarse.at[r, t, source],
            send_sem=ag_send.at[r, k],
            recv_sem=ag_recv.at[r, k],
            device_id=((c + k) % clusters, t),
            device_id_type=MESH,
        )

    def ag_start(r):
        @pl.loop(1, clusters)
        def _(k):
            ag_copy(r, k).start()

    def fwd_copy(r, which):
        return pltpu.make_async_remote_copy(
            src_ref=coarse.at[r, which],
            dst_ref=coarse.at[r, which],
            send_sem=fwd_send.at[r],
            recv_sem=fwd_recv.at[r],
            device_id=(c, other),
            device_id_type=MESH,
        )

    def ag_forward(r):
        @pl.loop(1, clusters)
        def _(k):
            ag_arrival(r, k).wait_recv()

        fwd_copy(r, t).start()

    def ag_finish(r):
        @pl.loop(1, clusters)
        def _(k):
            ag_copy(r, k).wait_send()

        fwd_copy(r, t).wait_send()
        fwd_copy(r, other).wait_recv()
        gathered = coarse[r].reshape(2 * clusters * 16, LANES)
        out = mm(near_cat[...], split(gathered))
        high, low = halves(fold(out[:LANES]) + out[LANES:, :LANES])
        wide = jnp.concatenate(
            [jnp.concatenate([high, low], axis=1), jnp.concatenate([high, jnp.zeros_like(high)], axis=1)],
            axis=0,
        )
        return wide, jnp.sum(gathered.reshape(2 * clusters, 16, LANES), axis=0)

    for n in range(BUFS):
        load(n, n).start()

    near[...] = jnp.zeros_like(near)
    barrier = pltpu.get_barrier_semaphore()

    @pl.loop(1, clusters)
    def _(k):
        pl.semaphore_signal(barrier, inc=1, device_id=((c + k) % clusters, t), device_id_type=MESH)

    pl.semaphore_signal(barrier, inc=1, device_id=(c, other), device_id_type=MESH)
    reached = [(has_up, up), (has_down, down), (has_up2, up2), (has_down2, down2)]
    for condition, cluster in reached:
        @pl.when(condition)
        def _(cluster=cluster):
            pl.semaphore_signal(barrier, inc=1, device_id=(cluster, other), device_id_type=MESH)

    rhs_copy = pltpu.make_async_copy(rhs_hbm, past, rhs_sem)
    rhs_copy.start()

    @pl.when(c == 0)
    def _():
        for r in range(HALOS):
            pool[r, 256:448, :] = jnp.zeros((192, LANES), F32)
            pool[r, 640:704, :] = jnp.zeros((64, LANES), F32)

    @pl.when(c == clusters - 1)
    def _():
        for r in range(HALOS):
            pool[r, 448:640, :] = jnp.zeros((192, LANES), F32)
            pool[r, 704:768, :] = jnp.zeros((64, LANES), F32)

    modes[...] = jnp.zeros_like(modes)
    for k in range(modes_in.shape[0]):
        modes[2 * k : 2 * k + 1, :rows] = modes_in[k, 0:1, :]
        modes[2 * k + 1 : 2 * k + 2, rows:] = modes_in[k, 1:2, :]

    def spread_tile(start):
        narrow = jnp.concatenate([modes[:, start : start + TILE], jnp.zeros((LANES - 16, TILE), F32)], axis=0)
        image[start : start + TILE, :] = pltpu.roll(jnp.transpose(narrow), slot * count, 1)

    for start in edges:
        spread_tile(start)

    coarse[0, t, c] = jnp.zeros((16, LANES), F32)
    for k in range(crhs.shape[0]):
        coarse[0, t, c, 2 * k : 2 * k + 2, :] = crhs[k]
    near[slot] = cinv[...]

    @pl.loop(0, inner // TILE)
    def _(n):
        at = lax.broadcasted_iota(jnp.int32, (TILE, inner), 0) + n * TILE
        perm0[n] = (at == members[1, 1:2, ESUB:] - ESUB).astype(F32).astype(BF16)
        perm1[n] = (at == members[0, 1:2, ESUB:] - (rows + ESUB)).astype(F32).astype(BF16)

    names = jnp.concatenate([members[0, :, :ESUB], members[1, :, :ESUB]], axis=1)
    offset = names - 2 * rows
    block = lax.shift_right_arithmetic(offset, 9)
    within = offset & (2 * ESUB - 1)
    cluster = lax.shift_right_arithmetic(block, 1)
    own = (block & 1) == t
    sibling = jnp.where(within < 128, within, within - 256)
    lower = jnp.where(own, jnp.where(within < 256, within + 128, within), within + 256)
    upper = jnp.where(own, jnp.where(within < 384, within + 192, within + 128), within + 256)
    place = jnp.where(cluster == 0, lower, jnp.where(cluster == 1, sibling, upper))
    named = names < 2 * rows + 12 * ESUB
    place = jnp.where(named, place, -1).astype(F32)
    size = jnp.sum(named.astype(F32), axis=0, keepdims=True)
    row = lax.broadcasted_iota(jnp.int32, place.shape, 0)
    outer[...] = jnp.zeros_like(outer)
    outer[0:4, :] = jnp.where(row == 0, 1.0 / size, place)
    columns[...] = jnp.transpose(outer[...])
    at = lax.broadcasted_iota(jnp.int32, (2 * ESUB, POOL), 1).astype(F32)
    hits = jnp.zeros((2 * ESUB, POOL), F32)
    for n in range(1, 4):
        hits = hits + (at == columns[:, n : n + 1]).astype(F32)
    share[...] = hits.astype(BF16)

    pl.semaphore_wait(barrier, clusters + (up - down) + (up2 - c) // 2 + (c - down2) // 2)

    start_all(halo_copies(image, 0))
    start_all(near_copies())
    ag_start(0)

    for start in inners:
        spread_tile(start)

    @pl.loop(0, 2 * per)
    def _(chunk):
        buf = chunk % BUFS
        sub, start = chunk_home(chunk)
        load(chunk, buf).wait()

        @pl.loop(0, TILE // 64)
        def _(n):
            value = ops_buf[buf, pl.ds(pl.multiple_of(n * 64, 64), 64), :]
            high, low = halves(value)
            at_rows = pl.ds(pl.multiple_of(start + n * 64, 64), 64)
            ops_hi[sub, at_rows, :] = high
            ops_lo[sub, at_rows, :] = low

        @pl.when(chunk + BUFS < 2 * per)
        def _():
            load(chunk + BUFS, buf).start()

    def tile(start, size=TILE):
        return pl.ds(start, size)

    def jump_inner(source, cat, emit):
        for n in range(inner // TILE):
            start = ESUB + n * TILE
            picked = fold(mm(perm0[n], cat[rows + ESUB : total, :]))
            emit(start, 0.5 * (source[tile(start), :] - picked))
            back = fold(mm(perm1[n], cat[ESUB:rows, :]))
            emit(rows + start, 0.5 * (source[tile(rows + start), :] - back))

    def jump_edge(source, r, emit):
        picked = fold(mm(share[...], split(pool[r])))
        scale = columns[:, 0:1]
        for n, start in enumerate(edges):
            at = slice(n * ESUB, (n + 1) * ESUB)
            value = source[tile(start), :]
            emit(start, value - (value + picked[at]) * scale[at])

    def product(sub, start, size, cat):
        at = pl.ds(start, size)
        whole = pl.ds(pl.multiple_of(sub * rows, TILE), rows)
        return fold(mm(ops_hi[sub, at, :], cat[whole, :])) + mm(ops_lo[sub, at, :], cat[whole, :LANES])

    def product_edges(source_cat, target, target_cat):
        for sub, start in enumerate(edges):
            out = product(sub, 0, ESUB, source_cat)
            target[tile(start), :] = out
            if target_cat is not None:
                target_cat[tile(start), :] = split(out)

    def product_rest(source_cat, target, target_cat):
        half = inner // 2

        @pl.loop(0, 4)
        def _(n):
            sub = n // 2
            start = pl.multiple_of(ESUB + (n % 2) * half, 128)
            out = product(sub, start, half, source_cat)
            at = pl.ds(pl.multiple_of(sub * rows + start, 128), half)
            target[at, :] = out
            target_cat[at, :] = split(out)

    def restrict(cat):
        out = mm(jnp.concatenate(halves(modes[...]), axis=0), cat[...])
        return fold(out[:16]) + out[16:, :LANES]

    def put(r, terms, sums):
        row = lax.broadcasted_iota(jnp.int32, (16, LANES), 0)
        for n, value in enumerate(sums):
            terms = jnp.where(row == count + n, value, terms)
        coarse[r, t, c] = terms

    def lift(basis, start, wide):
        return fold(mm(basis[tile(start), :], wide))

    for start in (*edges, *inners):
        cat[tile(start), :] = split(image[tile(start), :])

    def store_lift(start, value):
        lift_cat[tile(start), :] = split(value)

    jump_inner(image, cat, store_lift)
    wait_all(halo_copies(image, 0))
    jump_edge(image, 0, store_lift)
    ag_forward(0)
    product_edges(lift_cat, image, image_cat)

    wait_all(near_copies())
    for start in range(0, near_cat.shape[1], 512):
        at = slice(start, start + 512)
        parts = [near[which, :count, at] for which in range(2 * REACH)]
        parts.append(jnp.zeros((LANES - 2 * REACH * count, 512), F32))
        high, low = halves(jnp.concatenate(parts, axis=0))
        near_cat[:LANES, at] = high
        near_cat[LANES:, at] = low
    wide, _ = ag_finish(0)

    def start_tile(start):
        value = past[tile(start), :] - lift(image_cat, start, wide)
        field[tile(start), :] = value
        cat[tile(start), :] = split(value)

    rhs_copy.wait()
    for start in edges:
        start_tile(start)
    start_all(halo_copies(field, 2))
    start_all(halo_copies(image, 1))
    product_rest(lift_cat, image, image_cat)
    for start in inners:
        start_tile(start)

    def store_jumped(start, value):
        jumped[tile(start), :] = value
        cat2[tile(start), :] = split(value)

    jump_inner(field, cat, store_jumped)
    wait_all(halo_copies(field, 2))
    jump_edge(field, 2, store_jumped)
    put(1, restrict(cat2), [])
    ag_start(1)

    product_edges(cat2, field, None)
    start_all(halo_copies(field, 3))
    for start in (*edges, *inners):
        mult[tile(start), :] = lift(lift_cat, start, wide)

    def store_c1(start, value):
        c1_cat[tile(start), :] = split(value)

    jump_inner(image, image_cat, store_c1)
    product_rest(cat2, field, cat)
    wait_all(halo_copies(image, 1))
    jump_edge(image, 1, store_c1)
    ag_forward(1)
    wide, _ = ag_finish(1)
    zero = jnp.zeros((1, LANES), F32)
    sums = [zero, zero]

    def first_tile(start, value):
        along = value - lift(c1_cat, start, wide)
        now = jumped[tile(start), :] - lift(lift_cat, start, wide)
        proj[tile(start), :] = now
        past[tile(start), :] = along
        cat2[tile(start), :] = split(along)
        sums[0] = sums[0] + row_sum(now * along)
        sums[1] = sums[1] + row_sum(now * now)

    jump_inner(field, cat, first_tile)
    wait_all(halo_copies(field, 3))
    jump_edge(field, 3, first_tile)

    product_edges(cat2, image, None)
    start_all(halo_copies(image, 4))
    put(2, restrict(cat2), sums)
    ag_start(2)
    product_rest(cat2, image, cat)
    ag_forward(2)
    wide, totals = ag_finish(2)
    curvature, norm = totals[count : count + 1], totals[count + 1 : count + 2]
    step = norm / curvature
    sums = [zero, zero, zero]

    def second_tile(start, value):
        along = past[tile(start), :]
        old = proj[tile(start), :]
        moved = along - lift(lift_cat, start, wide)
        new = old - step * moved
        made = along - step * (value - lift(c1_cat, start, wide))
        mult[tile(start), :] = mult[tile(start), :] + step * old
        past[tile(start), :] = moved
        field[tile(start), :] = new
        jumped[tile(start), :] = made
        cat2[tile(start), :] = split(made)
        sums[0] = sums[0] + row_sum(new * made)
        sums[1] = sums[1] + row_sum(new * along + old * made)
        sums[2] = sums[2] + row_sum(new * new)

    jump_inner(image, cat, second_tile)
    wait_all(halo_copies(image, 4))
    jump_edge(image, 4, second_tile)
    put(3, restrict(cat2), sums)
    ag_start(3)
    ag_forward(3)
    wide, totals = ag_finish(3)
    fresh, crossed, norm_next = (totals[count + n : count + n + 1] for n in range(3))
    beta = norm_next / norm
    step_last = norm_next / (fresh + beta * (crossed + beta * curvature))

    for start in (*edges, *inners):
        new = field[tile(start), :]
        moved = jumped[tile(start), :] - lift(lift_cat, start, wide)
        mult[tile(start), :] = mult[tile(start), :] + step_last * (new + beta * proj[tile(start), :])
        proj[tile(start), :] = new - step_last * (moved + beta * past[tile(start), :])


def on_device(clusters, dual_ops, rigid_modes, members, coarse_inverse, dual_rhs, coarse_rhs):
    subs, rows, lanes = dual_rhs.shape
    modes_count = rigid_modes.shape[1]
    local_rows = subs * rows
    export = subs * ESUB
    inner = rows - ESUB

    count = subs * modes_count
    cinv = coarse_inverse.reshape(subs, modes_count, clusters, 2, subs, modes_count)
    cinv = cinv.transpose(1, 0, 3, 2, 5, 4).reshape(count, 2, clusters, count)
    cinv = jnp.pad(cinv, ((0, 16 - count), (0, 0), (0, 0), (0, 16 - count)))
    cinv = cinv.reshape(16, 2 * clusters * 16)

    vmem = pl.BlockSpec(memory_space=pltpu.VMEM)
    hbm = pl.BlockSpec(memory_space=pl.ANY)
    shape = jax.ShapeDtypeStruct((local_rows, lanes), F32)
    wide_cat = pltpu.VMEM((local_rows, 2 * lanes), BF16)
    whole = pltpu.VMEM((local_rows, lanes), F32)
    dma = pltpu.SemaphoreType.DMA
    mult, proj = pl.pallas_call(
        functools.partial(kernel, clusters=clusters),
        out_shape=(shape, shape),
        in_specs=[hbm, vmem, vmem, vmem, hbm, vmem],
        out_specs=(vmem, vmem),
        scratch_shapes=[
            pltpu.VMEM((subs, rows, rows), BF16),
            pltpu.VMEM((subs, rows, rows), BF16),
            pltpu.VMEM((BUFS, TILE, rows), F32),
            pltpu.VMEM((inner // TILE, TILE, inner), BF16),
            pltpu.VMEM((inner // TILE, TILE, inner), BF16),
            pltpu.VMEM((export, POOL), BF16),
            wide_cat, wide_cat, wide_cat, wide_cat, wide_cat,
            whole, whole, whole, whole,
            pltpu.VMEM((HALOS, POOL, lanes), F32),
            pltpu.VMEM((ROUNDS, 2, clusters, 16, lanes), F32),
            pltpu.VMEM((2 * REACH, 16, 2 * clusters * 16), F32),
            pltpu.VMEM((2 * LANES, 2 * clusters * 16), BF16),
            pltpu.VMEM((16, local_rows), F32),
            pltpu.VMEM((8, export), F32),
            pltpu.VMEM((export, 8), F32),
            dma((BUFS,)),
            dma,
            dma((HALOS, 8)),
            dma((HALOS, 8)),
            dma((9,)),
            dma((9,)),
            dma((ROUNDS, clusters)),
            dma((ROUNDS, clusters)),
            dma((ROUNDS,)),
            dma((ROUNDS,)),
        ],
        compiler_params=pltpu.CompilerParams(
            collective_id=0, has_side_effects=True, vmem_limit_bytes=60 * 2**20
        ),
    )(
        dual_ops, jnp.transpose(rigid_modes, (1, 0, 2)), members, cinv,
        dual_rhs.reshape(local_rows, lanes), jnp.transpose(coarse_rhs, (1, 0, 2)),
    )
    return mult.reshape(subs, rows, lanes), proj.reshape(subs, rows, lanes)


def solution(mesh):
    spec = P(("clus", "sub"), None, None)
    return jax.shard_map(
        functools.partial(on_device, mesh.shape["clus"]),
        mesh=mesh,
        in_specs=(spec, spec, spec, P(("clus", "sub"), None), spec, spec),
        out_specs=(spec, spec),
        check_vma=False,
    )
```

```python
import functools
import jax
import jax.numpy as jnp
from jax import lax
from jax.experimental import pallas as pl
from jax.experimental.pallas import tpu as pltpu
from jax.sharding import PartitionSpec as P

ESUB = 256
LANES = 128
TILE = 256
POOL = 768
ROUNDS = 4
HALOS = 5
BUFS = 4
HEAD = 32
BLOCK = 16
REACH = 5
MESH = pl.DeviceIdType.MESH
F32 = jnp.float32
BF16 = jnp.bfloat16


def halves(value):
    high = value.astype(BF16)
    return high, (value - high.astype(F32)).astype(BF16)


def split(value):
    return jnp.concatenate(halves(value), axis=1)


def mm(left, right):
    return jnp.dot(left, right, preferred_element_type=F32)


def fold(wide):
    return wide[:, :LANES] + wide[:, LANES:]


def row_sum(value):
    return jnp.sum(value, axis=0, keepdims=True)


def kernel(
    ops_hbm, modes_in, members, cinv_in, rhs_hbm, crhs,
    mult, proj,
    ops_hi, ops_lo, ops_buf, perm0, perm1, share, lift_cat, c1_cat, cat, cat2,
    image, field, jumped, past, pool, coarse, cinv, near, near_cat, modes, corners, outer, columns,
    ops_sem, rhs_sem, halo_send, halo_recv, near_send, near_recv, mode_send, mode_recv,
    ag_send, ag_recv, fwd_send, fwd_recv,
    *, clusters,
):
    c = lax.axis_index("clus")
    t = lax.axis_index("sub")
    other = 1 - t
    has_up = c < clusters - 1
    has_down = c > 0
    has_up2 = c < clusters - 2
    has_down2 = c > 1
    up = jnp.minimum(c + 1, clusters - 1)
    down = jnp.maximum(c - 1, 0)
    up2 = jnp.minimum(c + 2, clusters - 1)
    down2 = jnp.maximum(c - 2, 0)
    slot = (c % REACH) * 2 + t
    rows = ops_lo.shape[1]
    total = 2 * rows
    inner = rows - ESUB
    per = rows // TILE
    count = 2 * modes_in.shape[0]
    edges = (0, rows)
    inners = [start for n in range(1, per) for start in (n * TILE, rows + n * TILE)]

    def chunk_home(chunk):
        return chunk % 2, (chunk // 2) * TILE

    def load(chunk, buf):
        sub, start = chunk_home(chunk)
        return pltpu.make_async_copy(ops_hbm.at[sub, pl.ds(start, TILE)], ops_buf.at[buf], ops_sem.at[buf])

    def remote(source, target, sent, received, device):
        return pltpu.make_async_remote_copy(
            src_ref=source, dst_ref=target, send_sem=sent, recv_sem=received, device_id=device, device_id_type=MESH
        )

    def halo_copies(source, r):
        plan = [
            (0, 128, 0, (c, other)),
            (rows + 128, 128, 128, (c, other)),
            (rows + 128, 64, 384, (up, t)),
            (128, 128, 256, (up, t)),
            (rows + 192, 64, 576, (down, t)),
            (rows, 128, 448, (down, t)),
        ]
        copies = [
            remote(source.at[pl.ds(start, size)], pool.at[r, pl.ds(to, size)], halo_send.at[r, n], halo_recv.at[r, n], device)
            for n, (start, size, to, device) in enumerate(plan)
        ]
        onward = [
            remote(pool.at[r, pl.ds(start, 64)], pool.at[r, pl.ds(to, 64)], halo_send.at[r, n], halo_recv.at[r, n], (c, other))
            for n, start, to in ((6, 384, 640), (7, 576, 704))
        ]
        return copies, onward

    def halo_start(source, r):
        copies, _ = halo_copies(source, r)

        @pl.when(has_up)
        def _():
            copies[2].start()
            copies[3].start()

        @pl.when(has_down)
        def _():
            copies[4].start()
            copies[5].start()

        copies[0].start()
        copies[1].start()

    def halo_onward(source, r):
        copies, onward = halo_copies(source, r)

        @pl.when(has_down)
        def _():
            copies[2].wait_recv()
            onward[0].start()

        @pl.when(has_up)
        def _():
            copies[4].wait_recv()
            onward[1].start()

    def halo_wait(source, r):
        copies, onward = halo_copies(source, r)
        copies[0].wait()
        copies[1].wait()

        @pl.when(has_up)
        def _():
            copies[2].wait_send()
            copies[3].wait_send()
            copies[5].wait_recv()
            onward[1].wait()

        @pl.when(has_down)
        def _():
            copies[4].wait_send()
            copies[5].wait_send()
            copies[3].wait_recv()
            onward[0].wait()

    def mode_copies():
        low = rows + 128
        plan = [
            (0, (c, other)), (low, (c, other)),
            (128, (up, t)), (low, (up, t)), (low, (up, other)),
            (rows, (down, t)), (low, (down, t)), (low, (down, other)),
        ]
        copies = [
            remote(modes.at[:, pl.ds(start, 128)], corners.at[n], mode_send.at[n], mode_recv.at[n], device)
            for n, (start, device) in enumerate(plan)
        ]
        return [
            (None, None, copies[:2]),
            (has_up, has_down, copies[2:5]),
            (has_down, has_up, copies[5:]),
        ]

    def near_copies():
        plan = [
            (c, other), (up, t), (up, other), (down, t), (down, other),
            (up2, t), (up2, other), (down2, t), (down2, other),
        ]
        copies = [
            pltpu.make_async_remote_copy(
                src_ref=cinv,
                dst_ref=near.at[slot],
                send_sem=near_send.at[n],
                recv_sem=near_recv.at[n],
                device_id=device,
                device_id_type=MESH,
            )
            for n, device in enumerate(plan)
        ]
        return [
            (None, None, copies[:1]),
            (has_up, has_down, copies[1:3]),
            (has_down, has_up, copies[3:5]),
            (has_up2, has_down2, copies[5:7]),
            (has_down2, has_up2, copies[7:9]),
        ]

    def guarded(condition, action):
        if condition is None:
            action()
        else:
            pl.when(condition)(action)

    def start_all(groups):
        for sends, _, copies in reversed(groups):
            def go(copies=copies):
                for copy in copies:
                    copy.start()

            guarded(sends, go)

    def wait_all(groups):
        for sends, receives, copies in groups:
            def sent(copies=copies):
                for copy in copies:
                    copy.wait_send()

            def received(copies=copies):
                for copy in copies:
                    copy.wait_recv()

            guarded(sends, sent)
            guarded(receives, received)

    def ag_copy(r, k):
        return pltpu.make_async_remote_copy(
            src_ref=coarse.at[r, t, c],
            dst_ref=coarse.at[r, t, c],
            send_sem=ag_send.at[r, k],
            recv_sem=ag_recv.at[r, k],
            device_id=((c + k) % clusters, t),
            device_id_type=MESH,
        )

    def ag_arrival(r, k):
        source = (c + clusters - k) % clusters
        return pltpu.make_async_remote_copy(
            src_ref=coarse.at[r, t, source],
            dst_ref=coarse.at[r, t, source],
            send_sem=ag_send.at[r, k],
            recv_sem=ag_recv.at[r, k],
            device_id=((c + k) % clusters, t),
            device_id_type=MESH,
        )

    def ag_start(r):
        @pl.loop(1, clusters)
        def _(k):
            ag_copy(r, k).start()

    def fwd_copy(r, which):
        return pltpu.make_async_remote_copy(
            src_ref=coarse.at[r, which],
            dst_ref=coarse.at[r, which],
            send_sem=fwd_send.at[r],
            recv_sem=fwd_recv.at[r],
            device_id=(c, other),
            device_id_type=MESH,
        )

    def ag_forward(r):
        @pl.loop(1, clusters)
        def _(k):
            ag_arrival(r, k).wait_recv()

        fwd_copy(r, t).start()

    def ag_finish(r):
        @pl.loop(1, clusters)
        def _(k):
            ag_copy(r, k).wait_send()

        fwd_copy(r, t).wait_send()
        fwd_copy(r, other).wait_recv()
        gathered = coarse[r].reshape(2 * clusters * 16, LANES)
        out = mm(near_cat[...], split(gathered))
        high, low = halves(fold(out[:LANES]) + out[LANES:, :LANES])
        wide = jnp.concatenate(
            [jnp.concatenate([high, low], axis=1), jnp.concatenate([high, jnp.zeros_like(high)], axis=1)],
            axis=0,
        )
        return wide, jnp.sum(gathered.reshape(2 * clusters, 16, LANES), axis=0)

    for n in range(BUFS):
        load(n, n).start()

    barrier = pltpu.get_barrier_semaphore()

    @pl.loop(1, clusters)
    def _(k):
        pl.semaphore_signal(barrier, inc=1, device_id=((c + k) % clusters, t), device_id_type=MESH)

    pl.semaphore_signal(barrier, inc=1, device_id=(c, other), device_id_type=MESH)
    reached = [(has_up, up), (has_down, down), (has_up2, up2), (has_down2, down2)]
    for condition, cluster in reached:
        @pl.when(condition)
        def _(cluster=cluster):
            pl.semaphore_signal(barrier, inc=1, device_id=(cluster, other), device_id_type=MESH)

    rhs_copy = pltpu.make_async_copy(rhs_hbm, past, rhs_sem)
    rhs_copy.start()
    beyond = [(c < 1, REACH - 1), (c < 2, REACH - 2), (c > clusters - 2, 1), (c > clusters - 3, 2)]
    for missing, away in beyond:
        @pl.when(missing)
        def _(away=away):
            for u in range(2):
                near[(c + away) % REACH * 2 + u] = jnp.zeros(near.shape[1:], F32)


    @pl.when(c == 0)
    def _():
        for n in (2, 3, 4):
            corners[n] = jnp.zeros((16, 128), F32)
        for r in range(1, HALOS):
            pool[r, 256:448, :] = jnp.zeros((192, LANES), F32)
            pool[r, 640:704, :] = jnp.zeros((64, LANES), F32)

    @pl.when(c == clusters - 1)
    def _():
        for n in (5, 6, 7):
            corners[n] = jnp.zeros((16, 128), F32)
        for r in range(1, HALOS):
            pool[r, 448:640, :] = jnp.zeros((192, LANES), F32)
            pool[r, 704:768, :] = jnp.zeros((64, LANES), F32)

    modes[...] = jnp.zeros_like(modes)
    coarse[0, t, c] = jnp.zeros((16, LANES), F32)
    kinds = modes_in.shape[0]
    for k in range(kinds):
        for sub in range(2):
            at = kinds * sub + k
            modes[at : at + 1, sub * rows : (sub + 1) * rows] = modes_in[k, sub : sub + 1, :]
            coarse[0, t, c, at : at + 1, :] = crhs[k, sub : sub + 1, :]
    for sub in range(2):
        high, low = halves(modes[:, sub * rows : (sub + 1) * rows])
        ops_hi[sub, :16, :] = high
        ops_hi[sub, 16:HEAD, :] = low

    cinv[...] = jnp.zeros_like(cinv)
    whole = BLOCK * 2 * count
    at_in = lax.broadcasted_iota(jnp.int32, (whole, BLOCK * 16), 0)
    at_out = lax.broadcasted_iota(jnp.int32, (whole, BLOCK * 16), 1)
    inside = at_out & 15
    for n in range(clusters // BLOCK):
        value = cinv_in[:, n * whole : (n + 1) * whole]
        high, rest = value.astype(BF16), value - value.astype(BF16).astype(F32)
        middle, low = halves(rest)
        for u in range(2):
            home = (lax.shift_right_arithmetic(at_out, 4) * 2 + u) * count + inside
            pick = ((at_in == home) & (inside < count)).astype(F32).astype(BF16)
            start = u * clusters * 16 + n * BLOCK * 16
            cinv[:count, start : start + BLOCK * 16] = mm(high, pick) + (mm(middle, pick) + mm(low, pick))

    pl.semaphore_wait(barrier, clusters + (up - down) + (up2 - c) // 2 + (c - down2) // 2)

    start_all(mode_copies())
    ag_start(0)
    start_all(near_copies())
    rhs_copy.wait()
    halo_start(past, 1)

    near[slot] = cinv[...]

    @pl.loop(0, inner // TILE)
    def _(n):
        at = lax.broadcasted_iota(jnp.int32, (TILE, inner), 0) + n * TILE
        perm0[n] = (at == members[1, 1:2, ESUB:] - ESUB).astype(F32).astype(BF16)
        perm1[n] = (at == members[0, 1:2, ESUB:] - (rows + ESUB)).astype(F32).astype(BF16)

    names = jnp.concatenate([members[0, :, :ESUB], members[1, :, :ESUB]], axis=1)
    offset = names - 2 * rows
    block = lax.shift_right_arithmetic(offset, 9)
    within = offset & (2 * ESUB - 1)
    cluster = lax.shift_right_arithmetic(block, 1)
    own = (block & 1) == t
    sibling = jnp.where(within < 128, within, within - 256)
    lower = jnp.where(own, jnp.where(within < 256, within + 128, within), within + 256)
    upper = jnp.where(own, jnp.where(within < 384, within + 192, within + 128), within + 256)
    place = jnp.where(cluster == 0, lower, jnp.where(cluster == 1, sibling, upper))
    named = names < 2 * rows + 12 * ESUB
    place = jnp.where(named, place, -1).astype(F32)
    size = jnp.sum(named.astype(F32), axis=0, keepdims=True)
    row = lax.broadcasted_iota(jnp.int32, place.shape, 0)
    outer[...] = jnp.zeros_like(outer)
    outer[0:4, :] = jnp.where(row == 0, 1.0 / size, place)
    columns[...] = jnp.transpose(outer[...])
    at = lax.broadcasted_iota(jnp.int32, (2 * ESUB, POOL), 1).astype(F32)
    hits = jnp.zeros((2 * ESUB, POOL), F32)
    for n in range(1, 4):
        hits = hits + (at == columns[:, n : n + 1]).astype(F32)
    share[...] = hits.astype(BF16)

    def stand(narrow, shift):
        tall = jnp.concatenate([narrow, jnp.zeros((LANES - 16, narrow.shape[1]), F32)], axis=0)
        return pltpu.roll(jnp.transpose(tall), shift * count, 1)

    for start in (*edges, *inners):
        value = stand(modes[:, start : start + TILE], slot)
        image[start : start + TILE, :] = value
        cat[start : start + TILE, :] = split(value)

    def convert(chunk):
        buf = chunk % BUFS
        sub, start = chunk_home(chunk)
        load(chunk, buf).wait()
        for n in range(TILE // 64):
            high, low = halves(ops_buf[buf, n * 64 : (n + 1) * 64, :])
            ops_hi[sub, pl.ds(HEAD + start + n * 64, 64), :] = high
            ops_lo[sub, pl.ds(start + n * 64, 64), :] = low
        if chunk + BUFS < 2 * per:
            load(chunk + BUFS, buf).start()

    def tile(start, size=TILE):
        return pl.ds(start, size)

    def jump_inner(source, cat, emit):
        for n in range(inner // TILE):
            start = ESUB + n * TILE
            picked = fold(mm(perm0[n], cat[rows + ESUB : total, :]))
            emit(start, 0.5 * (source[tile(start), :] - picked))
            back = fold(mm(perm1[n], cat[ESUB:rows, :]))
            emit(rows + start, 0.5 * (source[tile(rows + start), :] - back))

    def jump_edge(source, r, emit):
        picked = fold(mm(share[...], split(pool[r])))
        scale = columns[:, 0:1]
        for n, start in enumerate(edges):
            at = slice(n * ESUB, (n + 1) * ESUB)
            value = source[tile(start), :]
            emit(start, value - (value + picked[at]) * scale[at])

    def product(sub, start, size, cat):
        high = pl.ds(pl.multiple_of(HEAD + start, HEAD), size)
        low = pl.ds(start, size)
        whole = pl.ds(pl.multiple_of(sub * rows, TILE), rows)
        return fold(mm(ops_hi[sub, high, :], cat[whole, :])) + mm(ops_lo[sub, low, :], cat[whole, :LANES])

    def coarse_terms(wide):
        return fold(wide[:16]) + wide[16:HEAD, :LANES]

    def product_edges(source_cat, target, target_cat):
        terms = jnp.zeros((16, LANES), F32)
        for sub, start in enumerate(edges):
            whole = slice(start, start + rows)
            wide = mm(ops_hi[sub, : HEAD + ESUB, :], source_cat[whole, :])
            terms = terms + coarse_terms(wide)
            out = fold(wide[HEAD:]) + mm(ops_lo[sub, :ESUB, :], source_cat[whole, :LANES])
            target[tile(start), :] = out
            if target_cat is not None:
                target_cat[tile(start), :] = split(out)
        return terms

    def product_rest(source_cat, target, target_cat):
        half = inner // 2

        @pl.loop(0, 4)
        def _(n):
            sub = n // 2
            start = pl.multiple_of(ESUB + (n % 2) * half, 128)
            out = product(sub, start, half, source_cat)
            at = pl.ds(pl.multiple_of(sub * rows + start, 128), half)
            target[at, :] = out
            target_cat[at, :] = split(out)

    def restrict(cat):
        return sum(
            coarse_terms(mm(ops_hi[sub, :HEAD, :], cat[start : start + rows, :])) for sub, start in enumerate(edges)
        )

    def put(r, terms, sums):
        row = lax.broadcasted_iota(jnp.int32, (16, LANES), 0)
        for n, value in enumerate(sums):
            terms = jnp.where(row == count + n, value, terms)
        coarse[r, t, c] = terms

    def lift(basis, start, wide):
        return fold(mm(basis[tile(start), :], wide))

    def store_lift(start, value):
        lift_cat[tile(start), :] = split(value)

    convert(0)
    jump_inner(image, cat, store_lift)
    convert(1)
    wait_all(mode_copies())
    below, above = (c + REACH - 1) % REACH, (c + 1) % REACH
    owners = [c % REACH * 2 + other] * 2 + [below * 2 + t] * 2 + [below * 2 + other]
    owners += [above * 2 + t] * 2 + [above * 2 + other]
    spots = [(0, 0, 128), (128, 0, 128), (256, 0, 128), (384, 0, 64), (640, 0, 64), (448, 0, 128), (576, 64, 64), (704, 64, 64)]
    for n, (to, start, size) in enumerate(spots):
        pool[0, to : to + size, :] = stand(corners[n], owners[n])[start : start + size]
    jump_edge(image, 0, store_lift)
    product_edges(lift_cat, image, cat)
    halo_start(image, 2)

    for chunk in range(2, 2 * per):
        convert(chunk)
        sub, start = chunk_home(chunk)
        out = product(sub, start, TILE, lift_cat)
        image[tile(sub * rows + start), :] = out
        cat[tile(sub * rows + start), :] = split(out)
        if chunk < 2 + len(edges):
            cat2[chunk % 2 * rows : (chunk % 2 + 1) * rows, :] = split(past[chunk % 2 * rows : (chunk % 2 + 1) * rows, :])

    def store_jumped(start, value):
        jumped[tile(start), :] = value

    jump_inner(past, cat2, store_jumped)
    halo_onward(past, 1)
    ag_forward(0)
    halo_onward(image, 2)
    wait_all(near_copies())
    for start in range(0, near_cat.shape[1], 512):
        at = slice(start, start + 512)
        parts = [near[which, :count, at] for which in range(2 * REACH)]
        parts.append(jnp.zeros((LANES - 2 * REACH * count, 512), F32))
        high, low = halves(jnp.concatenate(parts, axis=0))
        near_cat[:LANES, at] = high
        near_cat[LANES:, at] = low
    halo_wait(past, 1)
    jump_edge(past, 1, store_jumped)
    wide, _ = ag_finish(0)

    def start_tile(start, value):
        c1_cat[tile(start), :] = split(value)
        value = jumped[tile(start), :] - lift(c1_cat, start, wide)
        jumped[tile(start), :] = value
        cat2[tile(start), :] = split(value)

    jump_inner(image, cat, start_tile)
    halo_wait(image, 2)
    jump_edge(image, 2, start_tile)

    put(1, product_edges(cat2, field, None), [])
    ag_start(1)
    halo_start(field, 3)
    product_rest(cat2, field, cat)
    halo_onward(field, 3)
    for start in (*edges, *inners):
        mult[tile(start), :] = lift(lift_cat, start, wide)

    def store_along(start, value):
        past[tile(start), :] = value

    jump_inner(field, cat, store_along)
    ag_forward(1)
    halo_wait(field, 3)
    jump_edge(field, 3, store_along)
    wide, _ = ag_finish(1)
    zero = jnp.zeros((1, LANES), F32)
    sums = [zero, zero]

    def first_tile(start):
        along = past[tile(start), :] - lift(c1_cat, start, wide)
        now = jumped[tile(start), :] - lift(lift_cat, start, wide)
        proj[tile(start), :] = now
        past[tile(start), :] = along
        cat2[tile(start), :] = split(along)
        sums[0] = sums[0] + row_sum(now * along)
        sums[1] = sums[1] + row_sum(now * now)

    for start in (*edges, *inners):
        first_tile(start)

    put(2, product_edges(cat2, image, None), sums)
    ag_start(2)
    halo_start(image, 4)
    product_rest(cat2, image, cat)
    halo_onward(image, 4)

    def store_image(start, value):
        field[tile(start), :] = value

    jump_inner(image, cat, store_image)
    ag_forward(2)
    halo_wait(image, 4)
    jump_edge(image, 4, store_image)
    wide, totals = ag_finish(2)
    curvature, norm = totals[count : count + 1], totals[count + 1 : count + 2]
    step = norm / curvature
    sums = [zero, zero, zero]

    def second_tile(start):
        value = field[tile(start), :]
        along = past[tile(start), :]
        old = proj[tile(start), :]
        moved = along - lift(lift_cat, start, wide)
        new = old - step * moved
        made = along - step * (value - lift(c1_cat, start, wide))
        mult[tile(start), :] = mult[tile(start), :] + step * old
        past[tile(start), :] = moved
        field[tile(start), :] = new
        jumped[tile(start), :] = made
        cat2[tile(start), :] = split(made)
        sums[0] = sums[0] + row_sum(new * made)
        sums[1] = sums[1] + row_sum(new * along + old * made)
        sums[2] = sums[2] + row_sum(new * new)

    for start in (*edges, *inners):
        second_tile(start)

    put(3, restrict(cat2), sums)
    ag_start(3)
    ag_forward(3)
    wide, totals = ag_finish(3)
    fresh, crossed, norm_next = (totals[count + n : count + n + 1] for n in range(3))
    beta = norm_next / norm
    step_last = norm_next / (fresh + beta * (crossed + beta * curvature))

    for start in (*edges, *inners):
        new = field[tile(start), :]
        moved = jumped[tile(start), :] - lift(lift_cat, start, wide)
        mult[tile(start), :] = mult[tile(start), :] + step_last * (new + beta * proj[tile(start), :])
        proj[tile(start), :] = new - step_last * (moved + beta * past[tile(start), :])


def on_device(clusters, dual_ops, rigid_modes, members, coarse_inverse, dual_rhs, coarse_rhs):
    subs, rows, lanes = dual_rhs.shape
    modes_count = rigid_modes.shape[1]
    local_rows = subs * rows
    export = subs * ESUB
    inner = rows - ESUB

    vmem = pl.BlockSpec(memory_space=pltpu.VMEM)
    hbm = pl.BlockSpec(memory_space=pl.ANY)
    shape = jax.ShapeDtypeStruct((local_rows, lanes), F32)
    staged = pltpu.VMEM((local_rows, lanes), F32)
    wide_cat = pltpu.VMEM((local_rows, 2 * lanes), BF16)
    whole = pltpu.VMEM((local_rows, lanes), F32)
    dma = pltpu.SemaphoreType.DMA
    mult, proj = pl.pallas_call(
        functools.partial(kernel, clusters=clusters),
        out_shape=(staged, staged),
        in_specs=[hbm, vmem, vmem, vmem, hbm, vmem],
        out_specs=(vmem, vmem),
        scratch_shapes=[
            pltpu.VMEM((subs, HEAD + rows, rows), BF16),
            pltpu.VMEM((subs, rows, rows), BF16),
            pltpu.VMEM((BUFS, TILE, rows), F32),
            pltpu.VMEM((inner // TILE, TILE, inner), BF16),
            pltpu.VMEM((inner // TILE, TILE, inner), BF16),
            pltpu.VMEM((export, POOL), BF16),
            wide_cat, wide_cat, wide_cat, wide_cat,
            whole, whole, whole, whole,
            pltpu.VMEM((HALOS, POOL, lanes), F32),
            pltpu.VMEM((ROUNDS, 2, clusters, 16, lanes), F32),
            pltpu.VMEM((16, 2 * clusters * 16), F32),
            pltpu.VMEM((2 * REACH, 16, 2 * clusters * 16), F32),
            pltpu.VMEM((2 * LANES, 2 * clusters * 16), BF16),
            pltpu.VMEM((16, local_rows), F32),
            pltpu.VMEM((8, 16, LANES), F32),
            pltpu.VMEM((8, export), F32),
            pltpu.VMEM((export, 8), F32),
            dma((BUFS,)),
            dma,
            dma((HALOS, 8)),
            dma((HALOS, 8)),
            dma((9,)),
            dma((9,)),
            dma((8,)),
            dma((8,)),
            dma((ROUNDS, clusters)),
            dma((ROUNDS, clusters)),
            dma((ROUNDS,)),
            dma((ROUNDS,)),
        ],
        compiler_params=pltpu.CompilerParams(
            collective_id=0, has_side_effects=True, vmem_limit_bytes=60 * 2**20
        ),
    )(
        dual_ops, jnp.transpose(rigid_modes, (1, 0, 2)), members, coarse_inverse,
        dual_rhs.reshape(local_rows, lanes), jnp.transpose(coarse_rhs, (1, 0, 2)),
    )
    return mult.reshape(subs, rows, lanes), proj.reshape(subs, rows, lanes)


def solution(mesh):
    spec = P(("clus", "sub"), None, None)
    return jax.shard_map(
        functools.partial(on_device, mesh.shape["clus"]),
        mesh=mesh,
        in_specs=(spec, spec, spec, P(("clus", "sub"), None), spec, spec),
        out_specs=(spec, spec),
        check_vma=False,
    )
```

```python
import functools
import jax
import jax.numpy as jnp
from jax import lax
from jax.experimental import pallas as pl
from jax.experimental.pallas import tpu as pltpu
from jax.sharding import PartitionSpec as P

ESUB = 256
LANES = 128
TILE = 256
POOL = 768
ROUNDS = 4
HALOS = 5
BUFS = 4
HEAD = 32
BLOCK = 16
REACH = 5
MESH = pl.DeviceIdType.MESH
F32 = jnp.float32
BF16 = jnp.bfloat16


def halves(value):
    high = value.astype(BF16)
    return high, (value - high.astype(F32)).astype(BF16)


def split(value):
    return jnp.concatenate(halves(value), axis=1)


def mm(left, right):
    return jnp.dot(left, right, preferred_element_type=F32)


def fold(wide):
    return wide[:, :LANES] + wide[:, LANES:]


def row_sum(value):
    return jnp.sum(value, axis=0, keepdims=True)


def kernel(
    ops_hbm, modes_in, members, cinv_in, rhs_hbm, crhs,
    mult, proj,
    ops_hi, ops_lo, ops_buf, perm0, perm1, share, lift_cat, c1_cat, cat, cat2,
    image, field, jumped, past, pool, coarse, cinv, near, near_cat, held, modes, corners, outer, columns,
    ops_sem, rhs_sem, halo_send, halo_recv, near_send, near_recv, mode_send, mode_recv,
    ag_send, ag_recv, fwd_send, fwd_recv,
    *, clusters,
):
    c = lax.axis_index("clus")
    t = lax.axis_index("sub")
    other = 1 - t
    has_up = c < clusters - 1
    has_down = c > 0
    has_up2 = c < clusters - 2
    has_down2 = c > 1
    up = jnp.minimum(c + 1, clusters - 1)
    down = jnp.maximum(c - 1, 0)
    up2 = jnp.minimum(c + 2, clusters - 1)
    down2 = jnp.maximum(c - 2, 0)
    slot = (c % REACH) * 2 + t
    rows = ops_lo.shape[1]
    total = 2 * rows
    inner = rows - ESUB
    per = rows // TILE
    count = 2 * modes_in.shape[0]
    edges = (0, rows)
    inners = [start for n in range(1, per) for start in (n * TILE, rows + n * TILE)]

    def chunk_home(chunk):
        return chunk % 2, (chunk // 2) * TILE

    def load(chunk, buf):
        sub, start = chunk_home(chunk)
        return pltpu.make_async_copy(ops_hbm.at[sub, pl.ds(start, TILE)], ops_buf.at[buf], ops_sem.at[buf])

    def remote(source, target, sent, received, device):
        return pltpu.make_async_remote_copy(
            src_ref=source, dst_ref=target, send_sem=sent, recv_sem=received, device_id=device, device_id_type=MESH
        )

    def halo_copies(source, r):
        plan = [
            (0, 128, 0, (c, other)),
            (rows + 128, 128, 128, (c, other)),
            (rows + 128, 64, 384, (up, t)),
            (128, 128, 256, (up, t)),
            (rows + 192, 64, 576, (down, t)),
            (rows, 128, 448, (down, t)),
        ]
        copies = [
            remote(source.at[pl.ds(start, size)], pool.at[r, pl.ds(to, size)], halo_send.at[r, n], halo_recv.at[r, n], device)
            for n, (start, size, to, device) in enumerate(plan)
        ]
        onward = [
            remote(pool.at[r, pl.ds(start, 64)], pool.at[r, pl.ds(to, 64)], halo_send.at[r, n], halo_recv.at[r, n], (c, other))
            for n, start, to in ((6, 384, 640), (7, 576, 704))
        ]
        return copies, onward

    def halo_start(source, r):
        copies, _ = halo_copies(source, r)

        @pl.when(has_up)
        def _():
            copies[2].start()
            copies[3].start()

        @pl.when(has_down)
        def _():
            copies[4].start()
            copies[5].start()

        copies[0].start()
        copies[1].start()

    def halo_onward(source, r):
        copies, onward = halo_copies(source, r)

        @pl.when(has_down)
        def _():
            copies[2].wait_recv()
            onward[0].start()

        @pl.when(has_up)
        def _():
            copies[4].wait_recv()
            onward[1].start()

    def halo_wait(source, r):
        copies, onward = halo_copies(source, r)
        copies[0].wait()
        copies[1].wait()

        @pl.when(has_up)
        def _():
            copies[2].wait_send()
            copies[3].wait_send()
            copies[5].wait_recv()
            onward[1].wait()

        @pl.when(has_down)
        def _():
            copies[4].wait_send()
            copies[5].wait_send()
            copies[3].wait_recv()
            onward[0].wait()

    def mode_copies():
        low = rows + 128
        plan = [
            (0, (c, other)), (low, (c, other)),
            (128, (up, t)), (low, (up, t)), (low, (up, other)),
            (rows, (down, t)), (low, (down, t)), (low, (down, other)),
        ]
        copies = [
            remote(modes.at[:, pl.ds(start, 128)], corners.at[n], mode_send.at[n], mode_recv.at[n], device)
            for n, (start, device) in enumerate(plan)
        ]
        return [
            (None, None, copies[:2]),
            (has_up, has_down, copies[2:5]),
            (has_down, has_up, copies[5:]),
        ]

    def near_copies():
        plan = [
            (c, other), (up, t), (up, other), (down, t), (down, other),
            (up2, t), (up2, other), (down2, t), (down2, other),
        ]
        copies = [
            pltpu.make_async_remote_copy(
                src_ref=cinv,
                dst_ref=near.at[slot],
                send_sem=near_send.at[n],
                recv_sem=near_recv.at[n],
                device_id=device,
                device_id_type=MESH,
            )
            for n, device in enumerate(plan)
        ]
        return [
            (None, None, copies[:1]),
            (has_up, has_down, copies[1:3]),
            (has_down, has_up, copies[3:5]),
            (has_up2, has_down2, copies[5:7]),
            (has_down2, has_up2, copies[7:9]),
        ]

    def guarded(condition, action):
        if condition is None:
            action()
        else:
            pl.when(condition)(action)

    def start_all(groups):
        for sends, _, copies in reversed(groups):
            def go(copies=copies):
                for copy in copies:
                    copy.start()

            guarded(sends, go)

    def wait_all(groups):
        for sends, receives, copies in groups:
            def sent(copies=copies):
                for copy in copies:
                    copy.wait_send()

            def received(copies=copies):
                for copy in copies:
                    copy.wait_recv()

            guarded(sends, sent)
            guarded(receives, received)

    def ag_copy(r, k):
        return pltpu.make_async_remote_copy(
            src_ref=coarse.at[r, t, c],
            dst_ref=coarse.at[r, t, c],
            send_sem=ag_send.at[r, k],
            recv_sem=ag_recv.at[r, k],
            device_id=((c + k) % clusters, t),
            device_id_type=MESH,
        )

    def ag_arrival(r, k):
        source = (c + clusters - k) % clusters
        return pltpu.make_async_remote_copy(
            src_ref=coarse.at[r, t, source],
            dst_ref=coarse.at[r, t, source],
            send_sem=ag_send.at[r, k],
            recv_sem=ag_recv.at[r, k],
            device_id=((c + k) % clusters, t),
            device_id_type=MESH,
        )

    def ag_start(r):
        @pl.loop(1, clusters)
        def _(k):
            ag_copy(r, k).start()

    def fwd_copy(r, which):
        return pltpu.make_async_remote_copy(
            src_ref=coarse.at[r, which],
            dst_ref=coarse.at[r, which],
            send_sem=fwd_send.at[r],
            recv_sem=fwd_recv.at[r],
            device_id=(c, other),
            device_id_type=MESH,
        )

    def ag_forward(r):
        @pl.loop(1, clusters)
        def _(k):
            ag_arrival(r, k).wait_recv()

        fwd_copy(r, t).start()

    def ag_finish(r):
        @pl.loop(1, clusters)
        def _(k):
            ag_copy(r, k).wait_send()

        fwd_copy(r, t).wait_send()
        fwd_copy(r, other).wait_recv()
        gathered = coarse[r].reshape(2 * clusters * 16, LANES)
        out = mm(near_cat[...], split(gathered))
        high, low = halves(fold(out[:LANES]) + out[LANES:, :LANES])
        wide = jnp.concatenate(
            [jnp.concatenate([high, low], axis=1), jnp.concatenate([high, jnp.zeros_like(high)], axis=1)],
            axis=0,
        )
        return wide, jnp.sum(gathered.reshape(2 * clusters, 16, LANES), axis=0)

    for n in range(BUFS):
        load(n, n).start()

    barrier = pltpu.get_barrier_semaphore()

    @pl.loop(1, clusters)
    def _(k):
        pl.semaphore_signal(barrier, inc=1, device_id=((c + k) % clusters, t), device_id_type=MESH)

    pl.semaphore_signal(barrier, inc=1, device_id=(c, other), device_id_type=MESH)
    reached = [(has_up, up), (has_down, down), (has_up2, up2), (has_down2, down2)]
    for condition, cluster in reached:
        @pl.when(condition)
        def _(cluster=cluster):
            pl.semaphore_signal(barrier, inc=1, device_id=(cluster, other), device_id_type=MESH)

    rhs_copy = pltpu.make_async_copy(rhs_hbm, past, rhs_sem)
    rhs_copy.start()
    beyond = [(c < 1, REACH - 1), (c < 2, REACH - 2), (c > clusters - 2, 1), (c > clusters - 3, 2)]
    for missing, away in beyond:
        @pl.when(missing)
        def _(away=away):
            for u in range(2):
                near[(c + away) % REACH * 2 + u] = jnp.zeros(near.shape[1:], F32)


    @pl.when(c == 0)
    def _():
        for n in (2, 3, 4):
            corners[n] = jnp.zeros((16, 128), F32)
        for r in range(1, HALOS):
            pool[r, 256:448, :] = jnp.zeros((192, LANES), F32)
            pool[r, 640:704, :] = jnp.zeros((64, LANES), F32)

    @pl.when(c == clusters - 1)
    def _():
        for n in (5, 6, 7):
            corners[n] = jnp.zeros((16, 128), F32)
        for r in range(1, HALOS):
            pool[r, 448:640, :] = jnp.zeros((192, LANES), F32)
            pool[r, 704:768, :] = jnp.zeros((64, LANES), F32)

    modes[...] = jnp.zeros_like(modes)
    coarse[0, t, c] = jnp.zeros((16, LANES), F32)
    kinds = modes_in.shape[0]
    for k in range(kinds):
        for sub in range(2):
            at = kinds * sub + k
            modes[at : at + 1, sub * rows : (sub + 1) * rows] = modes_in[k, sub : sub + 1, :]
            coarse[0, t, c, at : at + 1, :] = crhs[k, sub : sub + 1, :]
    for sub in range(2):
        high, low = halves(modes[:, sub * rows : (sub + 1) * rows])
        ops_hi[sub, :16, :] = high
        ops_hi[sub, 16:HEAD, :] = low

    cinv[...] = jnp.zeros_like(cinv)
    whole = BLOCK * 2 * count
    at_in = lax.broadcasted_iota(jnp.int32, (whole, BLOCK * 16), 0)
    at_out = lax.broadcasted_iota(jnp.int32, (whole, BLOCK * 16), 1)
    inside = at_out & 15
    for n in range(clusters // BLOCK):
        value = cinv_in[:, n * whole : (n + 1) * whole]
        high, rest = value.astype(BF16), value - value.astype(BF16).astype(F32)
        middle, low = halves(rest)
        for u in range(2):
            home = (lax.shift_right_arithmetic(at_out, 4) * 2 + u) * count + inside
            pick = ((at_in == home) & (inside < count)).astype(F32).astype(BF16)
            start = u * clusters * 16 + n * BLOCK * 16
            cinv[:count, start : start + BLOCK * 16] = mm(high, pick) + (mm(middle, pick) + mm(low, pick))

    pl.semaphore_wait(barrier, clusters + (up - down) + (up2 - c) // 2 + (c - down2) // 2)

    start_all(mode_copies())
    ag_start(0)
    start_all(near_copies())
    rhs_copy.wait()
    halo_start(past, 1)

    @pl.loop(0, inner // TILE)
    def _(n):
        at = lax.broadcasted_iota(jnp.int32, (TILE, inner), 0) + n * TILE
        perm0[n] = (at == members[1, 1:2, ESUB:] - ESUB).astype(F32).astype(BF16)
        perm1[n] = (at == members[0, 1:2, ESUB:] - (rows + ESUB)).astype(F32).astype(BF16)

    names = jnp.concatenate([members[0, :, :ESUB], members[1, :, :ESUB]], axis=1)
    offset = names - 2 * rows
    block = lax.shift_right_arithmetic(offset, 9)
    within = offset & (2 * ESUB - 1)
    cluster = lax.shift_right_arithmetic(block, 1)
    own = (block & 1) == t
    sibling = jnp.where(within < 128, within, within - 256)
    lower = jnp.where(own, jnp.where(within < 256, within + 128, within), within + 256)
    upper = jnp.where(own, jnp.where(within < 384, within + 192, within + 128), within + 256)
    place = jnp.where(cluster == 0, lower, jnp.where(cluster == 1, sibling, upper))
    named = names < 2 * rows + 12 * ESUB
    place = jnp.where(named, place, -1).astype(F32)
    size = jnp.sum(named.astype(F32), axis=0, keepdims=True)
    row = lax.broadcasted_iota(jnp.int32, place.shape, 0)
    outer[...] = jnp.zeros_like(outer)
    outer[0:4, :] = jnp.where(row == 0, 1.0 / size, place)
    columns[...] = jnp.transpose(outer[...])
    at = lax.broadcasted_iota(jnp.int32, (2 * ESUB, POOL), 1).astype(F32)
    hits = jnp.zeros((2 * ESUB, POOL), F32)
    for n in range(1, 4):
        hits = hits + (at == columns[:, n : n + 1]).astype(F32)
    share[...] = hits.astype(BF16)

    def stand(narrow, shift):
        tall = jnp.concatenate([narrow, jnp.zeros((LANES - 16, narrow.shape[1]), F32)], axis=0)
        return pltpu.roll(jnp.transpose(tall), shift * count, 1)

    def convert(chunk):
        buf = chunk % BUFS
        sub, start = chunk_home(chunk)
        load(chunk, buf).wait()
        for n in range(TILE // 64):
            high, low = halves(ops_buf[buf, n * 64 : (n + 1) * 64, :])
            ops_hi[sub, pl.ds(HEAD + start + n * 64, 64), :] = high
            ops_lo[sub, pl.ds(start + n * 64, 64), :] = low
        if chunk + BUFS < 2 * per:
            load(chunk + BUFS, buf).start()

    def tile(start, size=TILE):
        return pl.ds(start, size)

    def jump_one(source, cat, emit, n, sub):
        start = sub * rows + ESUB + n * TILE
        apart = (1 - sub) * rows
        picked = fold(mm((perm0, perm1)[sub][n], cat[apart + ESUB : apart + rows, :]))
        emit(start, 0.5 * (source[tile(start), :] - picked))

    def jump_inner(source, cat, emit, subs=(0, 1)):
        for sub in subs:
            for n in range(inner // TILE):
                jump_one(source, cat, emit, n, sub)

    def jump_edge(source, r, emit):
        picked = fold(mm(share[...], split(pool[r])))
        scale = columns[:, 0:1]
        for n, start in enumerate(edges):
            at = slice(n * ESUB, (n + 1) * ESUB)
            value = source[tile(start), :]
            emit(start, value - (value + picked[at]) * scale[at])

    def product(sub, start, size, cat):
        high, low = slice(HEAD + start, HEAD + start + size), slice(start, start + size)
        whole = pl.ds(pl.multiple_of(sub * rows, TILE), rows)
        return fold(mm(ops_hi[sub, high, :], cat[whole, :])) + mm(ops_lo[sub, low, :], cat[whole, :LANES])

    def coarse_terms(wide):
        return fold(wide[:16]) + wide[16:HEAD, :LANES]

    def head_inner(cat, size):
        parts = []
        for sub, start in enumerate(edges):
            inner_at = slice(start + ESUB, start + rows)
            wide = mm(ops_hi[sub, : HEAD + size, ESUB:], cat[inner_at, :])
            part = None
            if size:
                part = fold(wide[HEAD:]) + mm(ops_lo[sub, :size, ESUB:], cat[inner_at, :LANES])
            parts.append((coarse_terms(wide), part))
        return parts

    def head_outer(cat, parts, emit):
        terms = jnp.zeros((16, LANES), F32)
        for sub, start in enumerate(edges):
            size = 0 if emit is None else ESUB
            wide = mm(ops_hi[sub, : HEAD + size, :ESUB], cat[tile(start), :])
            terms = terms + (parts[sub][0] + coarse_terms(wide))
            if emit is not None:
                out = fold(wide[HEAD:]) + mm(ops_lo[sub, :ESUB, :ESUB], cat[tile(start), :LANES])
                emit(start, out + parts[sub][1])
        return terms

    def product_rest(source_cat, target, target_cat):
        @pl.loop(0, 2)
        def _(sub):
            out = product(sub, ESUB, inner, source_cat)
            at = pl.ds(pl.multiple_of(sub * rows + ESUB, ESUB), inner)
            target[at, :] = out
            target_cat[at, :] = split(out)

    def put(r, terms, sums):
        row = lax.broadcasted_iota(jnp.int32, (16, LANES), 0)
        for n, value in enumerate(sums):
            terms = jnp.where(row == count + n, value, terms)
        coarse[r, t, c] = terms

    def lift(basis, start, wide):
        return fold(mm(basis[tile(start), :], wide))

    def store_lift(start, value):
        lift_cat[tile(start), :] = split(value)

    convert(0)
    for sub in range(2):
        own_at = slice(sub * rows + ESUB, (sub + 1) * rows)
        apart_at = slice((1 - sub) * rows + ESUB, (2 - sub) * rows)
        perm = (perm1, perm0)[sub][...].reshape(inner, inner)
        out = mm(jnp.concatenate(halves(modes[:, apart_at]), axis=0), perm)
        leaped = 0.5 * (modes[:, own_at] - (out[:16] + out[16:]))
        for n in range(inner // TILE):
            store_lift(sub * rows + ESUB + n * TILE, stand(leaped[:, n * TILE : (n + 1) * TILE], slot))
    for start in edges:
        image[tile(start), :] = stand(modes[:, start : start + TILE], slot)
    convert(1)
    parts = head_inner(lift_cat, ESUB)
    wait_all(mode_copies())
    below, above = (c + REACH - 1) % REACH, (c + 1) % REACH
    owners = [c % REACH * 2 + other] * 2 + [below * 2 + t] * 2 + [below * 2 + other]
    owners += [above * 2 + t] * 2 + [above * 2 + other]
    spots = [(0, 0, 128), (128, 0, 128), (256, 0, 128), (384, 0, 64), (640, 0, 64), (448, 0, 128), (576, 64, 64), (704, 64, 64)]
    for n, (to, start, size) in enumerate(spots):
        pool[0, to : to + size, :] = stand(corners[n], owners[n])[start : start + size]
    jump_edge(image, 0, store_lift)

    def store_image_edge(start, value):
        image[tile(start), :] = value
        cat[tile(start), :] = split(value)

    head_outer(lift_cat, parts, store_image_edge)
    halo_start(image, 2)

    near[slot] = cinv[...]

    def store_jumped(start, value):
        jumped[tile(start), :] = value

    for chunk in range(2, 2 * per):
        convert(chunk)
        sub, start = chunk_home(chunk)
        out = product(sub, start, TILE, lift_cat)
        image[tile(sub * rows + start), :] = out
        cat[tile(sub * rows + start), :] = split(out)
        if chunk < 4:
            at = slice(chunk % 2 * rows, (chunk % 2 + 1) * rows)
            cat2[at, :] = split(past[at, :])
    jump_inner(past, cat2, store_jumped)
    halo_onward(past, 1)
    ag_forward(0)
    wait_all(near_copies())
    for start in range(0, near_cat.shape[1], 512):
        at = slice(start, start + 512)
        parts = [near[which, :count, at] for which in range(2 * REACH)]
        parts.append(jnp.zeros((LANES - 2 * REACH * count, 512), F32))
        high, low = halves(jnp.concatenate(parts, axis=0))
        near_cat[:LANES, at] = high
        near_cat[LANES:, at] = low
    halo_onward(image, 2)
    halo_wait(past, 1)
    jump_edge(past, 1, store_jumped)
    wide, _ = ag_finish(0)
    held[...] = wide

    def start_tile(start, value):
        c1_cat[tile(start), :] = split(value)
        value = jumped[tile(start), :] - lift(c1_cat, start, wide)
        jumped[tile(start), :] = value
        cat2[tile(start), :] = split(value)

    jump_inner(image, cat, start_tile)
    parts = head_inner(cat2, ESUB)
    halo_wait(image, 2)
    jump_edge(image, 2, start_tile)


    def store_field_edge(start, value):
        field[tile(start), :] = value

    put(1, head_outer(cat2, parts, store_field_edge), [])
    ag_start(1)
    halo_start(field, 3)
    product_rest(cat2, field, cat)
    halo_onward(field, 3)
    def store_along(start, value):
        past[tile(start), :] = value

    jump_inner(field, cat, store_along, (0,))
    ag_forward(1)
    jump_inner(field, cat, store_along, (1,))
    wide, _ = ag_finish(1)
    zero = jnp.zeros((1, LANES), F32)
    sums = [zero, zero]

    def first_tile(start):
        along = past[tile(start), :] - lift(c1_cat, start, wide)
        now = jumped[tile(start), :] - lift(lift_cat, start, wide)
        proj[tile(start), :] = now
        past[tile(start), :] = along
        cat2[tile(start), :] = split(along)
        sums[0] = sums[0] + row_sum(now * along)
        sums[1] = sums[1] + row_sum(now * now)

    for start in inners:
        first_tile(start)
    parts = head_inner(cat2, ESUB)
    halo_wait(field, 3)
    jump_edge(field, 3, store_along)
    for start in edges:
        first_tile(start)


    def store_made_edge(start, value):
        image[tile(start), :] = value

    put(2, head_outer(cat2, parts, store_made_edge), sums)
    ag_start(2)
    halo_start(image, 4)
    product_rest(cat2, image, cat)
    halo_onward(image, 4)

    def store_image(start, value):
        field[tile(start), :] = value

    jump_inner(image, cat, store_image, (0,))
    ag_forward(2)
    jump_inner(image, cat, store_image, (1,))
    wide, totals = ag_finish(2)
    curvature, norm = totals[count : count + 1], totals[count + 1 : count + 2]
    step = norm / curvature
    sums = [zero, zero, zero]

    def second_tile(start):
        value = field[tile(start), :]
        along = past[tile(start), :]
        old = proj[tile(start), :]
        moved = along - lift(lift_cat, start, wide)
        new = old - step * moved
        made = along - step * (value - lift(c1_cat, start, wide))
        past[tile(start), :] = moved
        field[tile(start), :] = new
        jumped[tile(start), :] = made
        cat2[tile(start), :] = split(made)
        sums[0] = sums[0] + row_sum(new * made)
        sums[1] = sums[1] + row_sum(new * along + old * made)
        sums[2] = sums[2] + row_sum(new * new)

    for start in inners:
        second_tile(start)
    parts = head_inner(cat2, 0)
    halo_wait(image, 4)
    jump_edge(image, 4, store_image)
    for start in edges:
        second_tile(start)

    put(3, head_outer(cat2, parts, None), sums)
    ag_start(3)
    for start in (*edges, *inners):
        mult[tile(start), :] = lift(lift_cat, start, held[...]) + step * proj[tile(start), :]
    ag_forward(3)
    wide, totals = ag_finish(3)
    fresh, crossed, norm_next = (totals[count + n : count + n + 1] for n in range(3))
    beta = norm_next / norm
    step_last = norm_next / (fresh + beta * (crossed + beta * curvature))

    for start in (*edges, *inners):
        new = field[tile(start), :]
        moved = jumped[tile(start), :] - lift(lift_cat, start, wide)
        mult[tile(start), :] = mult[tile(start), :] + step_last * (new + beta * proj[tile(start), :])
        proj[tile(start), :] = new - step_last * (moved + beta * past[tile(start), :])


def on_device(clusters, dual_ops, rigid_modes, members, coarse_inverse, dual_rhs, coarse_rhs):
    subs, rows, lanes = dual_rhs.shape
    modes_count = rigid_modes.shape[1]
    local_rows = subs * rows
    export = subs * ESUB
    inner = rows - ESUB

    vmem = pl.BlockSpec(memory_space=pltpu.VMEM)
    hbm = pl.BlockSpec(memory_space=pl.ANY)
    shape = jax.ShapeDtypeStruct((local_rows, lanes), F32)
    staged = pltpu.VMEM((local_rows, lanes), F32)
    wide_cat = pltpu.VMEM((local_rows, 2 * lanes), BF16)
    whole = pltpu.VMEM((local_rows, lanes), F32)
    dma = pltpu.SemaphoreType.DMA
    mult, proj = pl.pallas_call(
        functools.partial(kernel, clusters=clusters),
        out_shape=(staged, staged),
        in_specs=[hbm, vmem, vmem, vmem, hbm, vmem],
        out_specs=(vmem, vmem),
        scratch_shapes=[
            pltpu.VMEM((subs, HEAD + rows, rows), BF16),
            pltpu.VMEM((subs, rows, rows), BF16),
            pltpu.VMEM((BUFS, TILE, rows), F32),
            pltpu.VMEM((inner // TILE, TILE, inner), BF16),
            pltpu.VMEM((inner // TILE, TILE, inner), BF16),
            pltpu.VMEM((export, POOL), BF16),
            wide_cat, wide_cat, wide_cat, wide_cat,
            whole, whole, whole, whole,
            pltpu.VMEM((HALOS, POOL, lanes), F32),
            pltpu.VMEM((ROUNDS, 2, clusters, 16, lanes), F32),
            pltpu.VMEM((16, 2 * clusters * 16), F32),
            pltpu.VMEM((2 * REACH, 16, 2 * clusters * 16), F32),
            pltpu.VMEM((2 * LANES, 2 * clusters * 16), BF16),
            pltpu.VMEM((2 * LANES, 2 * LANES), BF16),
            pltpu.VMEM((16, local_rows), F32),
            pltpu.VMEM((8, 16, LANES), F32),
            pltpu.VMEM((8, export), F32),
            pltpu.VMEM((export, 8), F32),
            dma((BUFS,)),
            dma,
            dma((HALOS, 8)),
            dma((HALOS, 8)),
            dma((9,)),
            dma((9,)),
            dma((8,)),
            dma((8,)),
            dma((ROUNDS, clusters)),
            dma((ROUNDS, clusters)),
            dma((ROUNDS,)),
            dma((ROUNDS,)),
        ],
        compiler_params=pltpu.CompilerParams(
            collective_id=0, has_side_effects=True, vmem_limit_bytes=60 * 2**20
        ),
    )(
        dual_ops, jnp.transpose(rigid_modes, (1, 0, 2)), members, coarse_inverse,
        dual_rhs.reshape(local_rows, lanes), jnp.transpose(coarse_rhs, (1, 0, 2)),
    )
    return mult.reshape(subs, rows, lanes), proj.reshape(subs, rows, lanes)


def solution(mesh):
    spec = P(("clus", "sub"), None, None)
    return jax.shard_map(
        functools.partial(on_device, mesh.shape["clus"]),
        mesh=mesh,
        in_specs=(spec, spec, spec, P(("clus", "sub"), None), spec, spec),
        out_specs=(spec, spec),
        check_vma=False,
    )
```

```python
import functools
import jax
import jax.numpy as jnp
from jax import lax
from jax.experimental import pallas as pl
from jax.experimental.pallas import tpu as pltpu
from jax.sharding import PartitionSpec as P

ESUB = 256
LANES = 128
TILE = 256
POOL = 768
ROUNDS = 4
HALOS = 5
BUFS = 4
HEAD = 32
BLOCK = 16
REACH = 5
MESH = pl.DeviceIdType.MESH
F32 = jnp.float32
BF16 = jnp.bfloat16


def halves(value):
    high = value.astype(BF16)
    return high, (value - high.astype(F32)).astype(BF16)


def split(value):
    return jnp.concatenate(halves(value), axis=1)


def mm(left, right):
    return jnp.dot(left, right, preferred_element_type=F32)


def fold(wide):
    return wide[:, :LANES] + wide[:, LANES:]


def row_sum(value):
    return jnp.sum(value, axis=0, keepdims=True)


def kernel(
    ops_hbm, modes_in, members, cinv_in, rhs_hbm, crhs,
    mult, proj,
    ops_hi, ops_lo, ops_buf, perm0, perm1, share, lift_cat, c1_cat, cat, cat2,
    image, field, jumped, past, pool, coarse, cinv, near, near_cat, held, modes, corners, outer, columns,
    ops_sem, rhs_sem, halo_send, halo_recv, near_send, near_recv, mode_send, mode_recv,
    ag_send, ag_recv, fwd_send, fwd_recv,
    *, clusters,
):
    c = lax.axis_index("clus")
    t = lax.axis_index("sub")
    other = 1 - t
    has_up = c < clusters - 1
    has_down = c > 0
    has_up2 = c < clusters - 2
    has_down2 = c > 1
    up = jnp.minimum(c + 1, clusters - 1)
    down = jnp.maximum(c - 1, 0)
    up2 = jnp.minimum(c + 2, clusters - 1)
    down2 = jnp.maximum(c - 2, 0)
    slot = (c % REACH) * 2 + t
    rows = ops_lo.shape[1]
    total = 2 * rows
    inner = rows - ESUB
    per = rows // TILE
    count = 2 * modes_in.shape[0]
    edges = (0, rows)
    inners = [start for n in range(1, per) for start in (n * TILE, rows + n * TILE)]

    def chunk_home(chunk):
        return chunk % 2, (chunk // 2) * TILE

    def load(chunk, buf):
        sub, start = chunk_home(chunk)
        return pltpu.make_async_copy(ops_hbm.at[sub, pl.ds(start, TILE)], ops_buf.at[buf], ops_sem.at[buf])

    def remote(source, target, sent, received, device):
        return pltpu.make_async_remote_copy(
            src_ref=source, dst_ref=target, send_sem=sent, recv_sem=received, device_id=device, device_id_type=MESH
        )

    def halo_copies(source, r):
        plan = [
            (0, 128, 0, (c, other)),
            (rows + 128, 128, 128, (c, other)),
            (rows + 128, 64, 384, (up, t)),
            (128, 128, 256, (up, t)),
            (rows + 192, 64, 576, (down, t)),
            (rows, 128, 448, (down, t)),
        ]
        copies = [
            remote(source.at[pl.ds(start, size)], pool.at[r, pl.ds(to, size)], halo_send.at[r, n], halo_recv.at[r, n], device)
            for n, (start, size, to, device) in enumerate(plan)
        ]
        onward = [
            remote(pool.at[r, pl.ds(start, 64)], pool.at[r, pl.ds(to, 64)], halo_send.at[r, n], halo_recv.at[r, n], (c, other))
            for n, start, to in ((6, 384, 640), (7, 576, 704))
        ]
        return copies, onward

    def halo_start(source, r):
        copies, _ = halo_copies(source, r)

        @pl.when(has_up)
        def _():
            copies[2].start()
            copies[3].start()

        @pl.when(has_down)
        def _():
            copies[4].start()
            copies[5].start()

        copies[0].start()
        copies[1].start()

    def halo_onward(source, r):
        copies, onward = halo_copies(source, r)

        @pl.when(has_down)
        def _():
            copies[2].wait_recv()
            onward[0].start()

        @pl.when(has_up)
        def _():
            copies[4].wait_recv()
            onward[1].start()

    def halo_wait(source, r):
        copies, onward = halo_copies(source, r)
        copies[0].wait()
        copies[1].wait()

        @pl.when(has_up)
        def _():
            copies[2].wait_send()
            copies[3].wait_send()
            copies[5].wait_recv()
            onward[1].wait()

        @pl.when(has_down)
        def _():
            copies[4].wait_send()
            copies[5].wait_send()
            copies[3].wait_recv()
            onward[0].wait()

    def mode_copies():
        low = rows + 128
        plan = [
            (0, (c, other)), (low, (c, other)),
            (128, (up, t)), (low, (up, t)), (low, (up, other)),
            (rows, (down, t)), (low, (down, t)), (low, (down, other)),
        ]
        copies = [
            remote(modes.at[:, pl.ds(start, 128)], corners.at[n], mode_send.at[n], mode_recv.at[n], device)
            for n, (start, device) in enumerate(plan)
        ]
        return [
            (None, None, copies[:2]),
            (has_up, has_down, copies[2:5]),
            (has_down, has_up, copies[5:]),
        ]

    def near_copies():
        plan = [
            (c, other), (up, t), (up, other), (down, t), (down, other),
            (up2, t), (up2, other), (down2, t), (down2, other),
        ]
        copies = [
            pltpu.make_async_remote_copy(
                src_ref=cinv,
                dst_ref=near.at[slot],
                send_sem=near_send.at[n],
                recv_sem=near_recv.at[n],
                device_id=device,
                device_id_type=MESH,
            )
            for n, device in enumerate(plan)
        ]
        return [
            (None, None, copies[:1]),
            (has_up, has_down, copies[1:3]),
            (has_down, has_up, copies[3:5]),
            (has_up2, has_down2, copies[5:7]),
            (has_down2, has_up2, copies[7:9]),
        ]

    def guarded(condition, action):
        if condition is None:
            action()
        else:
            pl.when(condition)(action)

    def start_all(groups):
        for sends, _, copies in reversed(groups):
            def go(copies=copies):
                for copy in copies:
                    copy.start()

            guarded(sends, go)

    def wait_all(groups):
        for sends, receives, copies in groups:
            def sent(copies=copies):
                for copy in copies:
                    copy.wait_send()

            def received(copies=copies):
                for copy in copies:
                    copy.wait_recv()

            guarded(sends, sent)
            guarded(receives, received)

    def ag_copy(r, k):
        return pltpu.make_async_remote_copy(
            src_ref=coarse.at[r, t, c],
            dst_ref=coarse.at[r, t, c],
            send_sem=ag_send.at[r, k],
            recv_sem=ag_recv.at[r, k],
            device_id=((c + k) % clusters, t),
            device_id_type=MESH,
        )

    def ag_arrival(r, k):
        source = (c + clusters - k) % clusters
        return pltpu.make_async_remote_copy(
            src_ref=coarse.at[r, t, source],
            dst_ref=coarse.at[r, t, source],
            send_sem=ag_send.at[r, k],
            recv_sem=ag_recv.at[r, k],
            device_id=((c + k) % clusters, t),
            device_id_type=MESH,
        )

    def ag_start(r):
        @pl.loop(1, clusters)
        def _(k):
            ag_copy(r, k).start()

    def fwd_copy(r, which):
        return pltpu.make_async_remote_copy(
            src_ref=coarse.at[r, which],
            dst_ref=coarse.at[r, which],
            send_sem=fwd_send.at[r],
            recv_sem=fwd_recv.at[r],
            device_id=(c, other),
            device_id_type=MESH,
        )

    def ag_forward(r):
        @pl.loop(1, clusters)
        def _(k):
            ag_arrival(r, k).wait_recv()

        fwd_copy(r, t).start()

    def ag_finish(r):
        @pl.loop(1, clusters)
        def _(k):
            ag_copy(r, k).wait_send()

        fwd_copy(r, t).wait_send()
        fwd_copy(r, other).wait_recv()
        gathered = coarse[r].reshape(2 * clusters * 16, LANES)
        out = mm(near_cat[...], split(gathered))
        high, low = halves(fold(out[:LANES]) + out[LANES:, :LANES])
        wide = jnp.concatenate(
            [jnp.concatenate([high, low], axis=1), jnp.concatenate([high, jnp.zeros_like(high)], axis=1)],
            axis=0,
        )
        return wide, jnp.sum(gathered.reshape(2 * clusters, 16, LANES), axis=0)

    for n in range(BUFS):
        load(n, n).start()

    barrier = pltpu.get_barrier_semaphore()

    @pl.loop(1, clusters)
    def _(k):
        pl.semaphore_signal(barrier, inc=1, device_id=((c + k) % clusters, t), device_id_type=MESH)

    pl.semaphore_signal(barrier, inc=1, device_id=(c, other), device_id_type=MESH)
    reached = [(has_up, up), (has_down, down), (has_up2, up2), (has_down2, down2)]
    for condition, cluster in reached:
        @pl.when(condition)
        def _(cluster=cluster):
            pl.semaphore_signal(barrier, inc=1, device_id=(cluster, other), device_id_type=MESH)

    rhs_copy = pltpu.make_async_copy(rhs_hbm, past, rhs_sem)
    rhs_copy.start()
    beyond = [(c < 1, REACH - 1), (c < 2, REACH - 2), (c > clusters - 2, 1), (c > clusters - 3, 2)]
    for missing, away in beyond:
        @pl.when(missing)
        def _(away=away):
            for u in range(2):
                near[(c + away) % REACH * 2 + u] = jnp.zeros(near.shape[1:], F32)


    @pl.when(c == 0)
    def _():
        for n in (2, 3, 4):
            corners[n] = jnp.zeros((16, 128), F32)
        for r in range(1, HALOS):
            pool[r, 256:448, :] = jnp.zeros((192, LANES), F32)
            pool[r, 640:704, :] = jnp.zeros((64, LANES), F32)

    @pl.when(c == clusters - 1)
    def _():
        for n in (5, 6, 7):
            corners[n] = jnp.zeros((16, 128), F32)
        for r in range(1, HALOS):
            pool[r, 448:640, :] = jnp.zeros((192, LANES), F32)
            pool[r, 704:768, :] = jnp.zeros((64, LANES), F32)

    modes[...] = jnp.zeros_like(modes)
    coarse[0, t, c] = jnp.zeros((16, LANES), F32)
    kinds = modes_in.shape[0]
    for k in range(kinds):
        for sub in range(2):
            at = kinds * sub + k
            modes[at : at + 1, sub * rows : (sub + 1) * rows] = modes_in[k, sub : sub + 1, :]
            coarse[0, t, c, at : at + 1, :] = crhs[k, sub : sub + 1, :]
    for sub in range(2):
        high, low = halves(modes[:, sub * rows : (sub + 1) * rows])
        ops_hi[sub, :16, :] = high
        ops_hi[sub, 16:HEAD, :] = low

    cinv[...] = jnp.zeros_like(cinv)
    whole = BLOCK * 2 * count
    at_in = lax.broadcasted_iota(jnp.int32, (whole, BLOCK * 16), 0)
    at_out = lax.broadcasted_iota(jnp.int32, (whole, BLOCK * 16), 1)
    inside = at_out & 15
    for n in range(clusters // BLOCK):
        value = cinv_in[:, n * whole : (n + 1) * whole]
        high, rest = value.astype(BF16), value - value.astype(BF16).astype(F32)
        middle, low = halves(rest)
        for u in range(2):
            home = (lax.shift_right_arithmetic(at_out, 4) * 2 + u) * count + inside
            pick = ((at_in == home) & (inside < count)).astype(F32).astype(BF16)
            start = u * clusters * 16 + n * BLOCK * 16
            cinv[:count, start : start + BLOCK * 16] = mm(high, pick) + (mm(middle, pick) + mm(low, pick))

    @pl.loop(0, inner // TILE)
    def _(n):
        at = lax.broadcasted_iota(jnp.int32, (TILE, inner), 0) + n * TILE
        perm0[n] = (at == members[1, 1:2, ESUB:] - ESUB).astype(F32).astype(BF16)
        perm1[n] = (at == members[0, 1:2, ESUB:] - (rows + ESUB)).astype(F32).astype(BF16)

    names = jnp.concatenate([members[0, :, :ESUB], members[1, :, :ESUB]], axis=1)
    offset = names - 2 * rows
    block = lax.shift_right_arithmetic(offset, 9)
    within = offset & (2 * ESUB - 1)
    cluster = lax.shift_right_arithmetic(block, 1)
    own = (block & 1) == t
    sibling = jnp.where(within < 128, within, within - 256)
    lower = jnp.where(own, jnp.where(within < 256, within + 128, within), within + 256)
    upper = jnp.where(own, jnp.where(within < 384, within + 192, within + 128), within + 256)
    place = jnp.where(cluster == 0, lower, jnp.where(cluster == 1, sibling, upper))
    named = names < 2 * rows + 12 * ESUB
    place = jnp.where(named, place, -1).astype(F32)
    size = jnp.sum(named.astype(F32), axis=0, keepdims=True)
    row = lax.broadcasted_iota(jnp.int32, place.shape, 0)
    outer[...] = jnp.zeros_like(outer)
    outer[0:4, :] = jnp.where(row == 0, 1.0 / size, place)
    columns[...] = jnp.transpose(outer[...])
    at = lax.broadcasted_iota(jnp.int32, (2 * ESUB, POOL), 1).astype(F32)
    hits = jnp.zeros((2 * ESUB, POOL), F32)
    for n in range(1, 4):
        hits = hits + (at == columns[:, n : n + 1]).astype(F32)
    share[...] = hits.astype(BF16)

    pl.semaphore_wait(barrier, clusters + (up - down) + (up2 - c) // 2 + (c - down2) // 2)

    start_all(mode_copies())
    ag_start(0)
    start_all(near_copies())
    rhs_copy.wait()
    halo_start(past, 1)

    def stand(narrow, shift):
        tall = jnp.concatenate([narrow, jnp.zeros((LANES - 16, narrow.shape[1]), F32)], axis=0)
        return pltpu.roll(jnp.transpose(tall), shift * count, 1)

    def convert(chunk):
        buf = chunk % BUFS
        sub, start = chunk_home(chunk)
        load(chunk, buf).wait()
        for n in range(TILE // 64):
            high, low = halves(ops_buf[buf, n * 64 : (n + 1) * 64, :])
            ops_hi[sub, pl.ds(HEAD + start + n * 64, 64), :] = high
            ops_lo[sub, pl.ds(start + n * 64, 64), :] = low
        if chunk + BUFS < 2 * per:
            load(chunk + BUFS, buf).start()

    def tile(start, size=TILE):
        return pl.ds(start, size)

    def jump_one(source, cat, emit, n, sub):
        start = sub * rows + ESUB + n * TILE
        apart = (1 - sub) * rows
        picked = fold(mm((perm0, perm1)[sub][n], cat[apart + ESUB : apart + rows, :]))
        emit(start, 0.5 * (source[tile(start), :] - picked))

    def jump_inner(source, cat, emit, subs=(0, 1)):
        for sub in subs:
            for n in range(inner // TILE):
                jump_one(source, cat, emit, n, sub)

    def jump_edge(source, r, emit):
        picked = fold(mm(share[...], split(pool[r])))
        scale = columns[:, 0:1]
        for n, start in enumerate(edges):
            at = slice(n * ESUB, (n + 1) * ESUB)
            value = source[tile(start), :]
            emit(start, value - (value + picked[at]) * scale[at])

    def product(sub, start, size, cat):
        high, low = slice(HEAD + start, HEAD + start + size), slice(start, start + size)
        whole = pl.ds(pl.multiple_of(sub * rows, TILE), rows)
        return fold(mm(ops_hi[sub, high, :], cat[whole, :])) + mm(ops_lo[sub, low, :], cat[whole, :LANES])

    def coarse_terms(wide):
        return fold(wide[:16]) + wide[16:HEAD, :LANES]

    def head_inner(cat, size):
        parts = []
        for sub, start in enumerate(edges):
            inner_at = slice(start + ESUB, start + rows)
            wide = mm(ops_hi[sub, : HEAD + size, ESUB:], cat[inner_at, :])
            part = None
            if size:
                part = fold(wide[HEAD:]) + mm(ops_lo[sub, :size, ESUB:], cat[inner_at, :LANES])
            parts.append((coarse_terms(wide), part))
        return parts

    def head_outer(cat, parts, emit):
        terms = jnp.zeros((16, LANES), F32)
        for sub, start in enumerate(edges):
            size = 0 if emit is None else ESUB
            wide = mm(ops_hi[sub, : HEAD + size, :ESUB], cat[tile(start), :])
            terms = terms + (parts[sub][0] + coarse_terms(wide))
            if emit is not None:
                out = fold(wide[HEAD:]) + mm(ops_lo[sub, :ESUB, :ESUB], cat[tile(start), :LANES])
                emit(start, out + parts[sub][1])
        return terms

    def product_rest(source_cat, target, target_cat):
        @pl.loop(0, 2)
        def _(sub):
            out = product(sub, ESUB, inner, source_cat)
            at = pl.ds(pl.multiple_of(sub * rows + ESUB, ESUB), inner)
            target[at, :] = out
            target_cat[at, :] = split(out)

    def put(r, terms, sums):
        row = lax.broadcasted_iota(jnp.int32, (16, LANES), 0)
        for n, value in enumerate(sums):
            terms = jnp.where(row == count + n, value, terms)
        coarse[r, t, c] = terms

    def lift(basis, start, wide):
        return fold(mm(basis[tile(start), :], wide))

    def store_lift(start, value):
        lift_cat[tile(start), :] = split(value)

    convert(0)
    for sub in range(2):
        own_at = slice(sub * rows + ESUB, (sub + 1) * rows)
        apart_at = slice((1 - sub) * rows + ESUB, (2 - sub) * rows)
        perm = (perm1, perm0)[sub][...].reshape(inner, inner)
        out = mm(jnp.concatenate(halves(modes[:, apart_at]), axis=0), perm)
        leaped = 0.5 * (modes[:, own_at] - (out[:16] + out[16:]))
        for n in range(inner // TILE):
            store_lift(sub * rows + ESUB + n * TILE, stand(leaped[:, n * TILE : (n + 1) * TILE], slot))
    for start in edges:
        image[tile(start), :] = stand(modes[:, start : start + TILE], slot)
    convert(1)
    parts = head_inner(lift_cat, ESUB)
    wait_all(mode_copies())
    below, above = (c + REACH - 1) % REACH, (c + 1) % REACH
    owners = [c % REACH * 2 + other] * 2 + [below * 2 + t] * 2 + [below * 2 + other]
    owners += [above * 2 + t] * 2 + [above * 2 + other]
    spots = [(0, 0, 128), (128, 0, 128), (256, 0, 128), (384, 0, 64), (640, 0, 64), (448, 0, 128), (576, 64, 64), (704, 64, 64)]
    for n, (to, start, size) in enumerate(spots):
        pool[0, to : to + size, :] = stand(corners[n], owners[n])[start : start + size]
    jump_edge(image, 0, store_lift)

    def store_image_edge(start, value):
        image[tile(start), :] = value
        cat[tile(start), :] = split(value)

    head_outer(lift_cat, parts, store_image_edge)
    halo_start(image, 2)

    near[slot] = cinv[...]

    def store_jumped(start, value):
        jumped[tile(start), :] = value

    for chunk in range(2, 2 * per):
        convert(chunk)
        sub, start = chunk_home(chunk)
        out = product(sub, start, TILE, lift_cat)
        image[tile(sub * rows + start), :] = out
        cat[tile(sub * rows + start), :] = split(out)
        if chunk < 4:
            at = slice(chunk % 2 * rows, (chunk % 2 + 1) * rows)
            cat2[at, :] = split(past[at, :])
    jump_inner(past, cat2, store_jumped)
    halo_onward(past, 1)
    ag_forward(0)
    wait_all(near_copies())
    for start in range(0, near_cat.shape[1], 512):
        at = slice(start, start + 512)
        parts = [near[which, :count, at] for which in range(2 * REACH)]
        parts.append(jnp.zeros((LANES - 2 * REACH * count, 512), F32))
        high, low = halves(jnp.concatenate(parts, axis=0))
        near_cat[:LANES, at] = high
        near_cat[LANES:, at] = low
    halo_onward(image, 2)
    halo_wait(past, 1)
    jump_edge(past, 1, store_jumped)
    wide, _ = ag_finish(0)
    held[...] = wide

    def start_tile(start, value):
        c1_cat[tile(start), :] = split(value)
        value = jumped[tile(start), :] - lift(c1_cat, start, wide)
        jumped[tile(start), :] = value
        cat2[tile(start), :] = split(value)

    jump_inner(image, cat, start_tile)
    parts = head_inner(cat2, ESUB)
    halo_wait(image, 2)
    jump_edge(image, 2, start_tile)


    def store_field_edge(start, value):
        field[tile(start), :] = value

    put(1, head_outer(cat2, parts, store_field_edge), [])
    ag_start(1)
    halo_start(field, 3)
    product_rest(cat2, field, cat)
    halo_onward(field, 3)
    def store_along(start, value):
        past[tile(start), :] = value

    ag_forward(1)
    jump_inner(field, cat, store_along)
    wide, _ = ag_finish(1)
    zero = jnp.zeros((1, LANES), F32)
    sums = [zero, zero]

    def first_tile(start):
        along = past[tile(start), :] - lift(c1_cat, start, wide)
        now = jumped[tile(start), :] - lift(lift_cat, start, wide)
        proj[tile(start), :] = now
        past[tile(start), :] = along
        cat2[tile(start), :] = split(along)
        sums[0] = sums[0] + row_sum(now * along)
        sums[1] = sums[1] + row_sum(now * now)

    for start in inners:
        first_tile(start)
    parts = head_inner(cat2, ESUB)
    halo_wait(field, 3)
    jump_edge(field, 3, store_along)
    for start in edges:
        first_tile(start)


    def store_made_edge(start, value):
        image[tile(start), :] = value

    put(2, head_outer(cat2, parts, store_made_edge), sums)
    ag_start(2)
    halo_start(image, 4)
    product_rest(cat2, image, cat)
    halo_onward(image, 4)

    def store_image(start, value):
        field[tile(start), :] = value

    ag_forward(2)
    jump_inner(image, cat, store_image)
    wide, totals = ag_finish(2)
    curvature, norm = totals[count : count + 1], totals[count + 1 : count + 2]
    step = norm / curvature
    sums = [zero, zero, zero]

    def second_tile(start):
        value = field[tile(start), :]
        along = past[tile(start), :]
        old = proj[tile(start), :]
        moved = along - lift(lift_cat, start, wide)
        new = old - step * moved
        made = along - step * (value - lift(c1_cat, start, wide))
        past[tile(start), :] = moved
        field[tile(start), :] = new
        jumped[tile(start), :] = made
        cat2[tile(start), :] = split(made)
        sums[0] = sums[0] + row_sum(new * made)
        sums[1] = sums[1] + row_sum(new * along + old * made)
        sums[2] = sums[2] + row_sum(new * new)

    for start in inners:
        second_tile(start)
    parts = head_inner(cat2, 0)
    halo_wait(image, 4)
    jump_edge(image, 4, store_image)
    for start in edges:
        second_tile(start)

    put(3, head_outer(cat2, parts, None), sums)
    ag_start(3)
    for start in (*edges, *inners):
        mult[tile(start), :] = lift(lift_cat, start, held[...]) + step * proj[tile(start), :]
    ag_forward(3)
    wide, totals = ag_finish(3)
    fresh, crossed, norm_next = (totals[count + n : count + n + 1] for n in range(3))
    beta = norm_next / norm
    step_last = norm_next / (fresh + beta * (crossed + beta * curvature))

    for start in (*edges, *inners):
        new = field[tile(start), :]
        moved = jumped[tile(start), :] - lift(lift_cat, start, wide)
        mult[tile(start), :] = mult[tile(start), :] + step_last * (new + beta * proj[tile(start), :])
        proj[tile(start), :] = new - step_last * (moved + beta * past[tile(start), :])


def on_device(clusters, dual_ops, rigid_modes, members, coarse_inverse, dual_rhs, coarse_rhs):
    subs, rows, lanes = dual_rhs.shape
    modes_count = rigid_modes.shape[1]
    local_rows = subs * rows
    export = subs * ESUB
    inner = rows - ESUB

    vmem = pl.BlockSpec(memory_space=pltpu.VMEM)
    hbm = pl.BlockSpec(memory_space=pl.ANY)
    shape = jax.ShapeDtypeStruct((local_rows, lanes), F32)
    staged = pltpu.VMEM((local_rows, lanes), F32)
    wide_cat = pltpu.VMEM((local_rows, 2 * lanes), BF16)
    whole = pltpu.VMEM((local_rows, lanes), F32)
    dma = pltpu.SemaphoreType.DMA
    mult, proj = pl.pallas_call(
        functools.partial(kernel, clusters=clusters),
        out_shape=(staged, staged),
        in_specs=[hbm, vmem, vmem, vmem, hbm, vmem],
        out_specs=(vmem, vmem),
        scratch_shapes=[
            pltpu.VMEM((subs, HEAD + rows, rows), BF16),
            pltpu.VMEM((subs, rows, rows), BF16),
            pltpu.VMEM((BUFS, TILE, rows), F32),
            pltpu.VMEM((inner // TILE, TILE, inner), BF16),
            pltpu.VMEM((inner // TILE, TILE, inner), BF16),
            pltpu.VMEM((export, POOL), BF16),
            wide_cat, wide_cat, wide_cat, wide_cat,
            whole, whole, whole, whole,
            pltpu.VMEM((HALOS, POOL, lanes), F32),
            pltpu.VMEM((ROUNDS, 2, clusters, 16, lanes), F32),
            pltpu.VMEM((16, 2 * clusters * 16), F32),
            pltpu.VMEM((2 * REACH, 16, 2 * clusters * 16), F32),
            pltpu.VMEM((2 * LANES, 2 * clusters * 16), BF16),
            pltpu.VMEM((2 * LANES, 2 * LANES), BF16),
            pltpu.VMEM((16, local_rows), F32),
            pltpu.VMEM((8, 16, LANES), F32),
            pltpu.VMEM((8, export), F32),
            pltpu.VMEM((export, 8), F32),
            dma((BUFS,)),
            dma,
            dma((HALOS, 8)),
            dma((HALOS, 8)),
            dma((9,)),
            dma((9,)),
            dma((8,)),
            dma((8,)),
            dma((ROUNDS, clusters)),
            dma((ROUNDS, clusters)),
            dma((ROUNDS,)),
            dma((ROUNDS,)),
        ],
        compiler_params=pltpu.CompilerParams(
            collective_id=0, has_side_effects=True, vmem_limit_bytes=60 * 2**20
        ),
    )(
        dual_ops, jnp.transpose(rigid_modes, (1, 0, 2)), members, coarse_inverse,
        dual_rhs.reshape(local_rows, lanes), jnp.transpose(coarse_rhs, (1, 0, 2)),
    )
    return mult.reshape(subs, rows, lanes), proj.reshape(subs, rows, lanes)


def solution(mesh):
    spec = P(("clus", "sub"), None, None)
    return jax.shard_map(
        functools.partial(on_device, mesh.shape["clus"]),
        mesh=mesh,
        in_specs=(spec, spec, spec, P(("clus", "sub"), None), spec, spec),
        out_specs=(spec, spec),
        check_vma=False,
    )
```
